768 devices in a mesh: ctx: 16 (over y, core), chan: 48 (over x, z).
Axes of the slice: x: 4, y: 8, z: 12, core: 2. Of those that a mesh axis runs over, the one named last changes fastest.
Arguments:
- queries: bfloat16 [1, 32768, 6144], P(None, 'ctx', 'chan')
- keys_in: bfloat16 [1, 32768, 6144], P(None, 'ctx', 'chan'), may hold values from -6 to 6
- values_in: bfloat16 [1, 32768, 6144], P(None, 'ctx', 'chan'), may hold values from -6 to 6
- short_weights: float32 [3, 7, 6144], P(None, None, 'chan'), may hold values from -2 to 2
- decay_rates: float32 [16, 6144], P(None, 'chan'), may hold values from 1.4953613e-06 to 0.0334, as said below
- residues: float32 [16, 6144], P(None, 'chan'), may hold values from -1.5 to 1.5
- skip_term: float32 [6144], P('chan'), may hold values from -1 to 1
- out_gain: float32 [6144], P('chan'), may hold values from 0.25 to 1.75
Outputs:
- normed: bfloat16 [1, 32768, 6144], P(None, 'ctx', 'chan')
The draws below stay inside these ranges and needn't reach their ends.
Inputs may be any that keep to these rules, and one draw needn't show every extreme that they name: `decay_rates`: each rate is positive.
All inputs are finite; a program needn't handle non-finite values.
Results may differ from the reference program's by a relative error of at most 0.0065.
Values may be sent and summed in bfloat16 or wider, within the bound.
A program may use at most 32 MiB of HBM per device.

```python
import math
import jax
import jax.numpy as jnp
from jax import lax

MODES = 16
KSHORT = 7
BLOCK = 128
SEQS = 1
LENGTH = 32768
CHANNELS = 6144


def draw_queries(key, part):
    base_key, col_key, row_key = jax.random.split(jax.random.fold_in(key, 11), 3)
    position = jnp.arange(CHANNELS).astype(jnp.float32) / CHANNELS
    column_scale = jnp.power(10.0, position) * jax.random.uniform(col_key, (CHANNELS,), jnp.float32, 0.7, 1.4)
    base = jnp.clip(jax.random.normal(base_key, (SEQS, LENGTH, CHANNELS), jnp.float32), -4.0, 4.0)
    row_scale = jnp.exp(jax.random.uniform(row_key, (SEQS, LENGTH, 1), jnp.float32, 0.0, math.log(10.0)))
    return (0.2 * base * row_scale * column_scale).astype(jnp.bfloat16)


def draw_decay_rates(key, part):
    slow_key, fast_key, pick_key = jax.random.split(jax.random.fold_in(key, 23), 3)
    slow = jnp.exp(jax.random.uniform(slow_key, (MODES, CHANNELS), jnp.float32, math.log(0.05), math.log(2.0))) / LENGTH
    fast = jnp.exp(jax.random.uniform(fast_key, (MODES, CHANNELS), jnp.float32, math.log(1.0 / 50.0), math.log(1.0 / 30.0)))
    share = 0.5
    chosen = jax.random.uniform(pick_key, (MODES, CHANNELS), jnp.float32) < share
    return jnp.where(chosen, fast, slow)


def block_scale(key, shape, cuts, low, top_value):
    level, own = 1.0, jax.random.fold_in(key, 6)
    for dim, blocks in cuts:
        draws = jnp.exp(jax.random.uniform(jax.random.fold_in(own, dim), (blocks,), jnp.float32, low / len(cuts), top_value / len(cuts)))
        level = level * jnp.repeat(draws, shape[dim] // blocks).reshape([-1 if axis == dim else 1 for axis in range(len(shape))])
    return level


def scatter_about(key, extent, deviation, reach, cuts=(), kind=jnp.bfloat16):
    array = deviation * jax.random.normal(key, extent, jnp.float32)
    if cuts:
        array = array * block_scale(key, extent, cuts, -0.22, 0.18)
    return jnp.clip(array, -reach, reach).astype(kind)


def setup_inputs(seed: int = 0) -> dict:
    key_list = jax.random.split(jax.random.key(seed), 9)
    queries = draw_queries(jax.random.fold_in(key_list[8], 71), 0)
    keys_in = scatter_about(key_list[1], (SEQS, LENGTH, CHANNELS), 1.0, 6.0, ((1, 16), (2, 48)))
    values_in = scatter_about(key_list[2], (SEQS, LENGTH, CHANNELS), 1.0, 6.0, ((1, 16), (2, 48)))
    short_weights = scatter_about(key_list[3], (3, KSHORT, CHANNELS), KSHORT ** -0.5, 2.0, ((2, 48),), jnp.float32)
    decay_rates = draw_decay_rates(jax.random.fold_in(key_list[8], 71), 0)
    residues = scatter_about(key_list[5], (MODES, CHANNELS), MODES ** -0.5, 1.5, ((1, 48),), jnp.float32)
    skip_term = jnp.clip(jax.random.uniform(key_list[6], (CHANNELS,), jnp.float32, -1.0, 1.0) * block_scale(key_list[6], (CHANNELS,), ((0, 48),), -0.4, 0.0), -1.0, 1.0)
    out_gain = jnp.clip(1.0 + 0.15 * jax.random.normal(key_list[7], (CHANNELS,), jnp.float32), 0.25, 1.75)
    return dict(queries=queries, keys_in=keys_in, values_in=values_in, short_weights=short_weights, decay_rates=decay_rates, residues=residues, skip_term=skip_term, out_gain=out_gain)


def short_filter(stream, taps):
    padded = jnp.pad(stream.astype(jnp.float32), ((0, 0), (KSHORT - 1, 0), (0, 0)))
    total = jnp.zeros(stream.shape, jnp.float32)
    for offset in range(KSHORT):
        total = total + taps[offset][None, None, :] * padded[:, KSHORT - 1 - offset:KSHORT - 1 - offset + LENGTH, :]
    return total

def link_states(earlier, later):
    return (earlier[0] * later[0], later[0] * earlier[1] + later[1])

def reference(queries, keys_in, values_in, short_weights, decay_rates, residues, skip_term, out_gain):
    qs = short_filter(queries, short_weights[0])
    ks = short_filter(keys_in, short_weights[1])
    vs = short_filter(values_in, short_weights[2])
    u_half = (ks * vs).astype(jnp.bfloat16)
    u_full = u_half.astype(jnp.float32)
    coef = residues * jnp.sqrt(-jnp.expm1(-2.0 * decay_rates))
    lag_list = jnp.arange(BLOCK).astype(jnp.float32)
    powers = jnp.exp(-decay_rates[:, None, :] * lag_list[None, :, None])
    filter_lags = lax.optimization_barrier(jnp.sum(coef[:, None, :] * powers, axis=0))
    index_diff = jnp.arange(BLOCK)[:, None] - jnp.arange(BLOCK)[None, :]
    lower = index_diff >= 0
    picked = filter_lags.T[:, jnp.maximum(index_diff, 0)]
    tile = jnp.where(lower[None, :, :], picked, 0.0).astype(jnp.bfloat16)
    block_count = LENGTH // BLOCK
    blocks = u_full.reshape(SEQS, block_count, BLOCK, CHANNELS)
    near = jnp.einsum('cij,snjc->snic', tile.astype(jnp.float32), blocks, precision=lax.Precision.HIGHEST)
    end_pow = jnp.exp(-decay_rates[:, None, :] * (BLOCK - 1 - lag_list)[None, :, None])
    ends = jnp.einsum('snjc,mjc->snmc', blocks, end_pow, precision=lax.Precision.HIGHEST)
    block_decay = jnp.broadcast_to(jnp.exp(-decay_rates * BLOCK)[None, None], ends.shape)
    _, inclusive = lax.associative_scan(link_states, (block_decay, ends), axis=1)
    start = jnp.concatenate([jnp.zeros_like(inclusive[:, :1]), inclusive[:, :-1]], axis=1)
    out_pow = coef[:, None, :] * jnp.exp(-decay_rates[:, None, :] * (lag_list + 1.0)[None, :, None])
    far = jnp.einsum('snmc,mic->snic', start, out_pow, precision=lax.Precision.HIGHEST)
    long_out = (near + far).reshape(SEQS, LENGTH, CHANNELS)
    mixed = qs * (long_out + skip_term * u_full)
    power = lax.optimization_barrier(jnp.mean(mixed * mixed, axis=-1, keepdims=True))
    return (mixed * lax.rsqrt(power + 1e-05) * out_gain).astype(jnp.bfloat16)
```

```python
import functools

import jax
import jax.numpy as jnp
from jax import lax
from jax.experimental import pallas as pl
from jax.experimental.pallas import tpu as pltpu
from jax.sharding import PartitionSpec as P

MESH = pl.DeviceIdType.MESH
F32 = jnp.float32
BF16 = jnp.bfloat16
SEG = 8
LANES = 128
UNROLL = 8
HALO = 16
X_CHIPS = 4


def expm1_of_minus(x):
    series = jnp.full_like(x, 1.0 / 40320.0)
    for factor in (5040.0, 720.0, 120.0, 24.0, 6.0, 2.0, 1.0):
        series = 1.0 / factor - x * series
    return jnp.where(x < 0.25, x * series, 1.0 - jnp.exp(-x))


def per_mode(rows):
    return jnp.broadcast_to(rows[:, None, :], (rows.shape[0], SEG, rows.shape[1]))


def body(
    sizes,
    q_hbm,
    k_hbm,
    v_hbm,
    w_hbm,
    lam_hbm,
    res_hbm,
    skip_hbm,
    gain_hbm,
    out_hbm,
    raw,
    nat,
    w_ref,
    lam_ref,
    res_ref,
    skip_ref,
    gain_ref,
    halo,
    u_ref,
    qs_ref,
    y_ref,
    mix_ref,
    pow_ref,
    send_state,
    got_state,
    send_x,
    got_x,
    send_z,
    got_z,
    out_v,
    in_sem,
    par_sem,
    halo_s,
    halo_r,
    st_s,
    st_r,
    x_s,
    x_r,
    z_s,
    z_r,
    out_sem,
):
    n_ctx, n_chan, width, taps, modes = sizes
    rows = q_hbm.shape[0]
    steps = rows // SEG
    z_chips = n_chan // X_CHIPS
    ctx = lax.axis_index("ctx")
    chan = lax.axis_index("chan")
    my_x, my_z = chan // z_chips, chan % z_chips

    def along_ctx(k):
        return ((ctx + k) % n_ctx, chan)

    def along_x(k):
        return (ctx, ((my_x + k) % X_CHIPS) * z_chips + my_z)

    def along_z(k):
        return (ctx, my_x * z_chips + (my_z + k) % z_chips)

    barrier = pltpu.get_barrier_semaphore()
    for k in range(1, n_ctx):
        pl.semaphore_signal(barrier, inc=1, device_id=along_ctx(k), device_id_type=MESH)
    for k in range(1, X_CHIPS):
        pl.semaphore_signal(barrier, inc=1, device_id=along_x(k), device_id_type=MESH)
    for k in range(1, z_chips):
        pl.semaphore_signal(barrier, inc=1, device_id=along_z(k), device_id_type=MESH)

    streams = (q_hbm, k_hbm, v_hbm)
    params = [
        pltpu.make_async_copy(src, dst, par_sem.at[i])
        for i, (src, dst) in enumerate(
            (
                (w_hbm, w_ref),
                (lam_hbm, lam_ref),
                (res_hbm, res_ref),
                (skip_hbm, skip_ref),
                (gain_hbm, gain_ref),
            )
        )
    ]
    loads = [pltpu.make_async_copy(streams[i], raw.at[i], in_sem.at[i]) for i in range(3)]
    loads[1].start()
    loads[2].start()
    for copy in params:
        copy.start()
    loads[0].start()
    for copy in params:
        copy.wait()

    lam = lam_ref[...]
    coef = res_ref[...] * jnp.sqrt(expm1_of_minus(2.0 * lam))
    decay = 1.0 - expm1_of_minus(lam)

    def to_natural(i):
        def convert(r, carry):
            start = pl.multiple_of(r * 64, 64)
            nat[i, pl.ds(8 + start, 64), :] = raw[i, pl.ds(start, 64), :].astype(F32)
            return carry

        lax.fori_loop(0, rows // 64, convert, 0)

    def tap(i, j):
        return jnp.broadcast_to(w_ref[i, j : j + 1, :], (SEG, width))

    def filtered(i, weights, t0):
        window = [
            nat[i, pl.ds(t0 + 2 + k + 7 - taps, SEG, stride=steps), :]
            for k in range(UNROLL + taps - 1)
        ]
        results = []
        for t in range(UNROLL):
            total = weights[0] * window[t + taps - 1]
            for j in range(1, taps):
                total = total + weights[j] * window[t + taps - 1 - j]
            results.append(total)
        return results

    loads[1].wait()
    to_natural(1)
    loads[2].wait()
    to_natural(2)

    w_k = [tap(1, j) for j in range(taps)]
    w_v = [tap(2, j) for j in range(taps)]

    def make_u(t0):
        ks = filtered(1, w_k, t0)
        vs = filtered(2, w_v, t0)
        for t in range(UNROLL):
            u_ref[t0 + t] = ks[t] * vs[t]

    def u_chunk(c, carry):
        make_u(pl.multiple_of(c * UNROLL, UNROLL))
        return carry

    lax.fori_loop(1, steps // UNROLL, u_chunk, 0)

    decay_b = per_mode(decay)

    def advance(t0, state):
        for t in range(UNROLL):
            state = decay_b * state + u_ref[t0 + t][None]
        return state

    def end_chunk(c, state):
        return advance(pl.multiple_of(c * UNROLL, UNROLL), state)

    zero_state = jnp.zeros((modes, SEG, width), F32)
    ends = lax.fori_loop(1, steps // UNROLL, end_chunk, zero_state)

    pl.semaphore_wait(barrier, (n_ctx - 1) + (X_CHIPS - 1) + (z_chips - 1))
    halos = [
        pltpu.make_async_remote_copy(
            src_ref=streams[i].at[pl.ds(rows - HALO, HALO)],
            dst_ref=halo.at[i],
            send_sem=halo_s.at[i],
            recv_sem=halo_r.at[i],
            device_id=along_ctx(1),
            device_id_type=MESH,
        )
        for i in range(3)
    ]
    for copy in halos:
        copy.start()
    loads[0].wait()
    to_natural(0)
    for copy in halos:
        copy.wait()
    has_before = (ctx > 0).astype(F32)
    for i in range(3):
        nat[i, 0:8, :] = halo[i].astype(F32)[8:16] * has_before

    make_u(0)
    first = advance(0, zero_state)
    ends = ends + per_mode(jnp.exp(lam * (-1.0 * (steps - UNROLL)))) * first

    segment = lax.broadcasted_iota(jnp.int32, (modes, SEG, width), 1)
    total = ends
    for shift in (1, 2, 4):
        weight = jnp.where(
            segment >= shift, per_mode(jnp.exp(lam * (-1.0 * steps * shift))), 0.0
        )
        total = total + weight * pltpu.roll(total, shift, 1)
    send_state[...] = total[:, SEG - 1, :].astype(BF16)
    start = jnp.where(segment >= 1, pltpu.roll(total, 1, 1), 0.0)

    states = [
        pltpu.make_async_remote_copy(
            src_ref=send_state,
            dst_ref=got_state.at[k],
            send_sem=st_s.at[k],
            recv_sem=st_r.at[k],
            device_id=along_ctx(k),
            device_id_type=MESH,
        )
        for k in range(1, n_ctx)
    ]
    for k in sorted(range(1, n_ctx), key=lambda k: abs(k - n_ctx // 2)):
        states[k - 1].start()

    w_q = [tap(0, j) for j in range(taps)]

    def q_chunk(c, carry):
        t0 = pl.multiple_of(c * UNROLL, UNROLL)
        qs = filtered(0, w_q, t0)
        for t in range(UNROLL):
            qs_ref[t0 + t] = qs[t]
        return carry

    lax.fori_loop(0, steps // UNROLL, q_chunk, 0)

    coef_b = per_mode(coef)
    skip_b = jnp.broadcast_to(skip_ref[...], (SEG, width))

    def y_chunk(c, state):
        t0 = pl.multiple_of(c * UNROLL, UNROLL)
        for t in range(UNROLL):
            u = u_ref[t0 + t]
            state = decay_b * state + u[None]
            y_ref[t0 + t] = jnp.sum(coef_b * state, axis=0) + skip_b * u
        return state

    lax.fori_loop(0, steps // UNROLL, y_chunk, start)

    device_decay = jnp.exp(lam * (-1.0 * rows))
    lead = per_mode(coef) * jnp.exp(
        per_mode(lam) * (-1.0 * steps * segment.astype(F32))
    )
    for copy in states:
        copy.wait()
    incoming = jnp.zeros((modes, width), F32)
    for k in range(n_ctx - 1, 0, -1):
        reached = (ctx >= k).astype(F32)
        incoming = device_decay * incoming + got_state[k].astype(F32) * reached

    def mix_chunk(c, far):
        t0 = pl.multiple_of(c * UNROLL, UNROLL)
        for t in range(UNROLL):
            far = decay_b * far
            mixed = qs_ref[t0 + t] * (y_ref[t0 + t] + jnp.sum(far, axis=0))
            mix_ref[pl.ds(t0 + t, SEG, stride=steps), :] = mixed
        return far

    lax.fori_loop(0, steps // UNROLL, mix_chunk, lead * per_mode(incoming))

    groups = rows // LANES
    ones = jnp.ones((2 * width, width), BF16)
    eye = (
        lax.broadcasted_iota(jnp.int32, (LANES, LANES), 0)
        == lax.broadcasted_iota(jnp.int32, (LANES, LANES), 1)
    )

    def power_group(g, carry):
        mixed = mix_ref[pl.ds(pl.multiple_of(g * LANES, LANES), LANES), :]
        square = mixed * mixed
        high = square.astype(BF16)
        low = (square - high.astype(F32)).astype(BF16)
        summed = jnp.dot(
            jnp.concatenate([high, low], axis=1), ones, preferred_element_type=F32
        )
        pow_ref[pl.ds(g, 1), :] = jnp.sum(jnp.where(eye, summed, 0.0), axis=0, keepdims=True)
        return carry

    lax.fori_loop(0, groups, power_group, 0)

    own = pow_ref[...]
    send_x[...] = own
    over_x = [
        pltpu.make_async_remote_copy(
            src_ref=send_x,
            dst_ref=got_x.at[k],
            send_sem=x_s.at[k],
            recv_sem=x_r.at[k],
            device_id=along_x(k),
            device_id_type=MESH,
        )
        for k in range(1, X_CHIPS)
    ]
    for copy in over_x:
        copy.start()
    for copy in over_x:
        copy.wait()
    own = own + sum(got_x[k] for k in range(1, X_CHIPS))
    send_z[...] = own.astype(BF16)
    over_z = [
        pltpu.make_async_remote_copy(
            src_ref=send_z,
            dst_ref=got_z.at[k],
            send_sem=z_s.at[k],
            recv_sem=z_r.at[k],
            device_id=along_z(k),
            device_id_type=MESH,
        )
        for k in range(1, z_chips)
    ]
    for k in sorted(range(1, z_chips), key=lambda k: abs(k - z_chips // 2)):
        over_z[k - 1].start()
    for copy in over_z:
        copy.wait()
    everything = own + sum(got_z[k].astype(F32) for k in range(1, z_chips))
    scale = lax.rsqrt(everything * (1.0 / (width * n_chan)) + 1e-05)

    padded = jnp.concatenate(
        [scale, jnp.zeros((LANES - groups, LANES), F32)], axis=0
    )
    columns = padded.T
    high = columns.astype(BF16)
    rest = columns - high.astype(F32)
    middle = rest.astype(BF16)
    low = (rest - middle.astype(F32)).astype(BF16)
    parts = jnp.concatenate([high, middle, low], axis=1)
    gain = gain_ref[...]
    part_row = lax.broadcasted_iota(jnp.int32, (3 * LANES, LANES), 0) % LANES

    outs = []
    for g in range(groups):
        pick = jnp.where(part_row == g, 1.0, 0.0).astype(BF16)
        spread = jnp.dot(parts, pick, preferred_element_type=F32)
        at = pl.ds(g * LANES, LANES)
        out_v[at, :] = (mix_ref[at, :] * spread * gain).astype(BF16)
        if g % 4 == 3:
            span = pl.ds((g - 3) * LANES, 4 * LANES)
            copy = pltpu.make_async_copy(out_v.at[span], out_hbm.at[span], out_sem.at[g // 4])
            copy.start()
            outs.append(copy)
    for copy in outs:
        copy.wait()


def shards(n_ctx, n_chan, queries, keys_in, values_in, short_weights, decay_rates, residues, skip_term, out_gain):
    rows, width = queries.shape[1:]
    taps, modes = short_weights.shape[1], decay_rates.shape[0]
    steps, groups = rows // SEG, rows // LANES
    z_chips = n_chan // X_CHIPS
    dma = pltpu.SemaphoreType.DMA
    out = pl.pallas_call(
        functools.partial(body, (n_ctx, n_chan, width, taps, modes)),
        out_shape=jax.ShapeDtypeStruct((rows, width), BF16),
        in_specs=[pl.BlockSpec(memory_space=pl.ANY)] * 8,
        out_specs=pl.BlockSpec(memory_space=pl.ANY),
        scratch_shapes=[
            pltpu.VMEM((3, rows, width), BF16),
            pltpu.VMEM((3, rows + 8, width), F32),
            pltpu.VMEM((3, taps, width), F32),
            pltpu.VMEM((modes, width), F32),
            pltpu.VMEM((modes, width), F32),
            pltpu.VMEM((1, width), F32),
            pltpu.VMEM((1, width), F32),
            pltpu.VMEM((3, HALO, width), BF16),
            pltpu.VMEM((steps, SEG, width), F32),
            pltpu.VMEM((steps, SEG, width), F32),
            pltpu.VMEM((steps, SEG, width), F32),
            pltpu.VMEM((rows, width), F32),
            pltpu.VMEM((groups, LANES), F32),
            pltpu.VMEM((modes, width), BF16),
            pltpu.VMEM((n_ctx, modes, width), BF16),
            pltpu.VMEM((groups, LANES), F32),
            pltpu.VMEM((X_CHIPS, groups, LANES), F32),
            pltpu.VMEM((groups, LANES), BF16),
            pltpu.VMEM((z_chips, groups, LANES), BF16),
            pltpu.VMEM((rows, width), BF16),
            dma((3,)),
            dma((5,)),
            dma((3,)),
            dma((3,)),
            dma((n_ctx,)),
            dma((n_ctx,)),
            dma((X_CHIPS,)),
            dma((X_CHIPS,)),
            dma((z_chips,)),
            dma((z_chips,)),
            dma((groups // 4,)),
        ],
        compiler_params=pltpu.CompilerParams(collective_id=0, has_side_effects=True),
        name="hyena",
    )(
        queries[0],
        keys_in[0],
        values_in[0],
        short_weights,
        decay_rates,
        residues,
        skip_term[None],
        out_gain[None],
    )
    return out[None]


def solution(mesh):
    placed = (
        P(None, "ctx", "chan"),
        P(None, "ctx", "chan"),
        P(None, "ctx", "chan"),
        P(None, None, "chan"),
        P(None, "chan"),
        P(None, "chan"),
        P("chan"),
        P("chan"),
    )
    return jax.shard_map(
        functools.partial(shards, mesh.shape["ctx"], mesh.shape["chan"]),
        mesh=mesh,
        in_specs=placed,
        out_specs=P(None, "ctx", "chan"),
        check_vma=False,
    )
```

```python
import functools

import jax
import jax.numpy as jnp
from jax import lax
from jax.experimental import pallas as pl
from jax.experimental.pallas import tpu as pltpu
from jax.sharding import PartitionSpec as P

MESH = pl.DeviceIdType.MESH
F32 = jnp.float32
BF16 = jnp.bfloat16
SEG = 8
LANES = 128
CHUNK = 16
KEPT = 4
HALO = 16
X_CHIPS = 4


def expm1_of_minus(x):
    series = jnp.full_like(x, 1.0 / 40320.0)
    for factor in (5040.0, 720.0, 120.0, 24.0, 6.0, 2.0, 1.0):
        series = 1.0 / factor - x * series
    return jnp.where(x < 0.25, x * series, 1.0 - jnp.exp(-x))


def per_mode(rows):
    return jnp.broadcast_to(rows[:, None, :], (rows.shape[0], SEG, rows.shape[1]))


def over_modes(terms):
    while terms.shape[0] > 1:
        half = terms.shape[0] // 2
        terms = terms[:half] + terms[half:]
    return terms[0]


def in_all(row):
    return jnp.broadcast_to(row, (SEG, row.shape[-1]))


def body(
    sizes,
    q_hbm,
    k_hbm,
    v_hbm,
    w_hbm,
    lam_hbm,
    res_hbm,
    skip_hbm,
    gain_hbm,
    mix_ref,
    sum_ref,
    raw,
    w_ref,
    lam_ref,
    res_ref,
    skip_ref,
    gain_ref,
    halo,
    u_ref,
    qs_ref,
    y_ref,
    kept,
    out_pow,
    send_state,
    got_state,
    send_x,
    got_x,
    send_z,
    got_z,
    in_sem,
    par_sem,
    halo_s,
    halo_r,
    st_s,
    st_r,
    x_s,
    x_r,
    z_s,
    z_r,
):
    n_ctx, n_chan, width, taps, modes = sizes
    rows = q_hbm.shape[0]
    steps = rows // SEG
    chunks = steps // CHUNK
    rim = taps - 1
    z_chips = n_chan // X_CHIPS
    ctx = lax.axis_index("ctx")
    chan = lax.axis_index("chan")
    my_x, my_z = chan // z_chips, chan % z_chips

    def along_ctx(k):
        return ((ctx + k) % n_ctx, chan)

    def along_x(k):
        return (ctx, ((my_x + k) % X_CHIPS) * z_chips + my_z)

    def along_z(k):
        return (ctx, my_x * z_chips + (my_z + k) % z_chips)

    barrier = pltpu.get_barrier_semaphore()
    for k in range(1, n_ctx):
        pl.semaphore_signal(barrier, inc=1, device_id=along_ctx(k), device_id_type=MESH)
    for k in range(1, X_CHIPS):
        pl.semaphore_signal(barrier, inc=1, device_id=along_x(k), device_id_type=MESH)
    for k in range(1, z_chips):
        pl.semaphore_signal(barrier, inc=1, device_id=along_z(k), device_id_type=MESH)

    streams = (q_hbm, k_hbm, v_hbm)
    params = [
        pltpu.make_async_copy(src, dst, par_sem.at[i])
        for i, (src, dst) in enumerate(
            (
                (w_hbm, w_ref),
                (lam_hbm, lam_ref),
                (res_hbm, res_ref),
                (skip_hbm, skip_ref),
                (gain_hbm, gain_ref),
            )
        )
    ]
    loads = [pltpu.make_async_copy(streams[i], raw.at[i], in_sem.at[i]) for i in range(3)]
    loads[1].start()
    loads[2].start()
    for copy in params:
        copy.start()
    loads[0].start()
    for copy in params:
        copy.wait()

    lam = lam_ref[...]
    coef = res_ref[...] * jnp.sqrt(expm1_of_minus(2.0 * lam))
    decay = 1.0 - expm1_of_minus(lam)
    decay_b = per_mode(decay)
    coef_b = per_mode(coef)

    def by_step(i, c):
        parts = [
            raw[i, pl.ds(pl.multiple_of(s * steps + c * CHUNK, CHUNK), CHUNK), :]
            for s in range(SEG)
        ]
        return jnp.swapaxes(jnp.stack(parts).astype(F32), 0, 1)

    def taps_of(i):
        return [in_all(w_ref[i, j : j + 1, :]) for j in range(taps)]

    def filtered(weights, window):
        total = weights[0][None] * window[rim:]
        for j in range(1, taps):
            total = total + weights[j][None] * window[rim - j : rim - j + CHUNK]
        return total

    def make_u(c, before_k, before_v):
        window_k = jnp.concatenate([before_k, by_step(1, c)], axis=0)
        window_v = jnp.concatenate([before_v, by_step(2, c)], axis=0)
        at = pl.ds(pl.multiple_of(c * CHUNK, CHUNK), CHUNK)
        u_ref[at] = filtered(w_k, window_k) * filtered(w_v, window_v)
        return window_k[CHUNK:], window_v[CHUNK:]

    def u_chunk(c, before):
        return make_u(c, *before)

    loads[1].wait()
    loads[2].wait()
    w_k, w_v = taps_of(1), taps_of(2)
    first_k, first_v = by_step(1, 0)[CHUNK - rim :], by_step(2, 0)[CHUNK - rim :]
    before = lax.fori_loop(1, chunks // 2, u_chunk, (first_k, first_v))

    pl.semaphore_wait(barrier, (n_ctx - 1) + (X_CHIPS - 1) + (z_chips - 1))
    halos = [
        pltpu.make_async_remote_copy(
            src_ref=streams[i].at[pl.ds(rows - HALO, HALO)],
            dst_ref=halo.at[i],
            send_sem=halo_s.at[i],
            recv_sem=halo_r.at[i],
            device_id=along_ctx(1),
            device_id_type=MESH,
        )
        for i in range(3)
    ]
    for copy in halos:
        copy.start()
    tail_k, tail_v = lax.fori_loop(chunks // 2, chunks, u_chunk, before)

    def advance(c, state):
        for t in range(CHUNK):
            at = c * CHUNK + t
            if t % KEPT == 0:
                kept[c * (CHUNK // KEPT) + t // KEPT] = state
            state = decay_b * state + u_ref[at][None]
        return state

    zero_state = jnp.zeros((modes, SEG, width), F32)
    ends = lax.fori_loop(1, chunks, advance, zero_state)

    for copy in halos:
        copy.wait()
    has_before = (ctx > 0).astype(F32)
    top = lax.broadcasted_iota(jnp.int32, (rim, SEG, width), 1) == 0

    def entering(i, tail):
        rows_before = halo[i].astype(F32)[HALO - rim :] * has_before
        spread = jnp.broadcast_to(rows_before[:, None, :], (rim, SEG, width))
        return jnp.where(top, spread, pltpu.roll(tail, 1, 1))

    make_u(0, entering(1, tail_k), entering(2, tail_v))
    first = advance(0, zero_state)
    ends = ends + per_mode(jnp.exp(lam * (-1.0 * (steps - CHUNK)))) * first

    segment = lax.broadcasted_iota(jnp.int32, (modes, SEG, width), 1)
    total = ends
    for shift in (1, 2, 4):
        weight = jnp.where(
            segment >= shift, per_mode(jnp.exp(lam * (-1.0 * steps * shift))), 0.0
        )
        total = total + weight * pltpu.roll(total, shift, 1)
    send_state[...] = total[:, SEG - 1, :].astype(BF16)
    start = jnp.where(segment >= 1, pltpu.roll(total, 1, 1), 0.0)

    states = [
        pltpu.make_async_remote_copy(
            src_ref=send_state,
            dst_ref=got_state.at[k],
            send_sem=st_s.at[k],
            recv_sem=st_r.at[k],
            device_id=along_ctx(k),
            device_id_type=MESH,
        )
        for k in range(1, n_ctx)
    ]
    for k in sorted(range(1, n_ctx), key=lambda k: abs(k - n_ctx // 2)):
        states[k - 1].start()

    loads[0].wait()
    w_q = taps_of(0)

    def q_chunk(c, before_q):
        window = jnp.concatenate([before_q, by_step(0, c)], axis=0)
        at = pl.ds(pl.multiple_of(c * CHUNK, CHUNK), CHUNK)
        qs_ref[at] = filtered(w_q, window)
        return window[CHUNK:]

    tail_q = by_step(0, chunks - 1)[CHUNK - rim :]
    lax.fori_loop(0, chunks, q_chunk, entering(0, tail_q))

    response = []
    power_of = coef
    for i in range(KEPT):
        response.append(in_all(jnp.sum(power_of, axis=0, keepdims=True)))
        power_of = power_of * decay
        out_pow[i] = per_mode(power_of)
    response[0] = response[0] + in_all(skip_ref[...])

    def y_chunk(c, carry):
        for b in range(CHUNK // KEPT):
            state = kept[c * (CHUNK // KEPT) + b]
            for i in range(KEPT):
                at = c * CHUNK + b * KEPT + i
                y = over_modes(out_pow[i] * state)
                for j in range(i + 1):
                    y = y + response[j] * u_ref[at - j]
                y_ref[at] = y
        return carry

    lax.fori_loop(0, chunks, y_chunk, 0)

    device_decay = jnp.exp(lam * (-1.0 * rows))
    lead = jnp.exp(per_mode(lam) * (-1.0 * steps * segment.astype(F32)))
    for copy in states:
        copy.wait()
    incoming = jnp.zeros((modes, width), F32)
    for k in range(n_ctx - 1, 0, -1):
        reached = (ctx >= k).astype(F32)
        incoming = device_decay * incoming + got_state[k].astype(F32) * reached

    lane = lax.broadcasted_iota(jnp.int32, (SEG, LANES), 1)
    half = chunks // 2
    gain = in_all(gain_ref[...])

    def mix_chunk(c, carry):
        far, power = carry
        place = lane - (c % half) * CHUNK
        for t in range(CHUNK):
            at = c * CHUNK + t
            far = decay_b * far
            mixed = qs_ref[at] * (y_ref[at] + over_modes(far))
            mix_ref[pl.ds(at, SEG, stride=steps), :] = mixed * gain
            power = jnp.where(
                place == t, jnp.sum(mixed * mixed, axis=1, keepdims=True), power
            )
        return far, power

    far = coef_b * (start + lead * per_mode(incoming))
    no_power = jnp.zeros((SEG, LANES), F32)
    far, power = mix_chunk(0, (far, no_power))
    far, power_0 = lax.fori_loop(1, half, mix_chunk, (far + coef_b * first, power))
    _, power_1 = lax.fori_loop(half, chunks, mix_chunk, (far, no_power))

    own = jnp.concatenate([power_0, power_1], axis=0)
    send_x[...] = own
    over_x = [
        pltpu.make_async_remote_copy(
            src_ref=send_x,
            dst_ref=got_x.at[k],
            send_sem=x_s.at[k],
            recv_sem=x_r.at[k],
            device_id=along_x(k),
            device_id_type=MESH,
        )
        for k in range(1, X_CHIPS)
    ]
    for copy in over_x:
        copy.start()
    for copy in over_x:
        copy.wait()
    own = own + sum(got_x[k] for k in range(1, X_CHIPS))
    send_z[...] = own.astype(BF16)
    over_z = [
        pltpu.make_async_remote_copy(
            src_ref=send_z,
            dst_ref=got_z.at[k],
            send_sem=z_s.at[k],
            recv_sem=z_r.at[k],
            device_id=along_z(k),
            device_id_type=MESH,
        )
        for k in range(1, z_chips)
    ]
    for copy in over_z:
        copy.start()
    for copy in over_z:
        copy.wait()
    sum_ref[...] = own + sum(got_z[k].astype(F32) for k in range(1, z_chips))


def finish(channels, mix_ref, sum_ref, out_hbm, out_v, out_sem):
    groups = sum_ref.shape[0]
    scale = lax.rsqrt(sum_ref[...] * (1.0 / channels) + 1e-05)
    padded = jnp.concatenate(
        [scale, jnp.zeros((LANES - groups, LANES), F32)], axis=0
    )
    columns = padded.T
    halves = groups // SEG
    outs = []
    for g in range(groups):
        row = (g % halves) * SEG + g // halves
        spread = jnp.broadcast_to(columns[:, row : row + 1], (LANES, LANES))
        at = pl.ds(g * LANES, LANES)
        out_v[at, :] = (mix_ref[at, :] * spread).astype(BF16)
        if g % 4 == 3:
            span = pl.ds((g - 3) * LANES, 4 * LANES)
            copy = pltpu.make_async_copy(out_v.at[span], out_hbm.at[span], out_sem.at[g // 4])
            copy.start()
            outs.append(copy)
    for copy in outs:
        copy.wait()


def shards(n_ctx, n_chan, queries, keys_in, values_in, short_weights, decay_rates, residues, skip_term, out_gain):
    rows, width = queries.shape[1:]
    taps, modes = short_weights.shape[1], decay_rates.shape[0]
    steps, groups = rows // SEG, rows // LANES
    z_chips = n_chan // X_CHIPS
    dma = pltpu.SemaphoreType.DMA
    vmem = pl.BlockSpec(memory_space=pltpu.VMEM)
    hbm = pl.BlockSpec(memory_space=pltpu.HBM)
    mixed, sums = pl.pallas_call(
        functools.partial(body, (n_ctx, n_chan, width, taps, modes)),
        out_shape=(
            jax.ShapeDtypeStruct((rows, width), F32),
            jax.ShapeDtypeStruct((groups, LANES), F32),
        ),
        in_specs=[hbm] * 8,
        out_specs=(vmem, vmem),
        scratch_shapes=[
            pltpu.VMEM((3, rows, width), BF16),
            pltpu.VMEM((3, taps, width), F32),
            pltpu.VMEM((modes, width), F32),
            pltpu.VMEM((modes, width), F32),
            pltpu.VMEM((1, width), F32),
            pltpu.VMEM((1, width), F32),
            pltpu.VMEM((3, HALO, width), BF16),
            pltpu.VMEM((steps, SEG, width), F32),
            pltpu.VMEM((steps, SEG, width), F32),
            pltpu.VMEM((steps, SEG, width), F32),
            pltpu.VMEM((steps // KEPT, modes, SEG, width), F32),
            pltpu.VMEM((KEPT, modes, SEG, width), F32),
            pltpu.VMEM((modes, width), BF16),
            pltpu.VMEM((n_ctx, modes, width), BF16),
            pltpu.VMEM((groups, LANES), F32),
            pltpu.VMEM((X_CHIPS, groups, LANES), F32),
            pltpu.VMEM((groups, LANES), BF16),
            pltpu.VMEM((z_chips, groups, LANES), BF16),
            dma((3,)),
            dma((5,)),
            dma((3,)),
            dma((3,)),
            dma((n_ctx,)),
            dma((n_ctx,)),
            dma((X_CHIPS,)),
            dma((X_CHIPS,)),
            dma((z_chips,)),
            dma((z_chips,)),
        ],
        compiler_params=pltpu.CompilerParams(
            collective_id=0, has_side_effects=True, vmem_limit_bytes=24 << 20
        ),
        name="hyena",
    )(
        *(
            pltpu.with_memory_space_constraint(x, pltpu.HBM)
            for x in (
                queries[0],
                keys_in[0],
                values_in[0],
                short_weights,
                decay_rates,
                residues,
                skip_term[None],
                out_gain[None],
            )
        )
    )
    out = pl.pallas_call(
        functools.partial(finish, width * n_chan),
        out_shape=jax.ShapeDtypeStruct((rows, width), BF16),
        in_specs=[vmem, vmem],
        out_specs=hbm,
        scratch_shapes=[pltpu.VMEM((rows, width), BF16), dma((groups // 4,))],
        compiler_params=pltpu.CompilerParams(vmem_limit_bytes=8 << 20),
        name="finish",
    )(mixed, sums)
    return out[None]


def solution(mesh):
    placed = (
        P(None, "ctx", "chan"),
        P(None, "ctx", "chan"),
        P(None, "ctx", "chan"),
        P(None, None, "chan"),
        P(None, "chan"),
        P(None, "chan"),
        P("chan"),
        P("chan"),
    )
    return jax.shard_map(
        functools.partial(shards, mesh.shape["ctx"], mesh.shape["chan"]),
        mesh=mesh,
        in_specs=placed,
        out_specs=P(None, "ctx", "chan"),
        check_vma=False,
    )
```

```python
import functools

import jax
import jax.numpy as jnp
from jax import lax
from jax.experimental import pallas as pl
from jax.experimental.pallas import tpu as pltpu
from jax.sharding import PartitionSpec as P

MESH = pl.DeviceIdType.MESH
F32 = jnp.float32
BF16 = jnp.bfloat16
SEG = 8
LANES = 128
CHUNK = 16
KEPT = 4
HALO = 16
X_CHIPS = 4


def expm1_of_minus(x):
    series = jnp.full_like(x, 1.0 / 40320.0)
    for factor in (5040.0, 720.0, 120.0, 24.0, 6.0, 2.0, 1.0):
        series = 1.0 / factor - x * series
    return jnp.where(x < 0.25, x * series, 1.0 - jnp.exp(-x))


def per_mode(rows):
    return jnp.broadcast_to(rows[:, None, :], (rows.shape[0], SEG, rows.shape[1]))


def over_modes(terms):
    while terms.shape[0] > 1:
        half = terms.shape[0] // 2
        terms = terms[:half] + terms[half:]
    return terms[0]


def in_all(row):
    return jnp.broadcast_to(row, (SEG, row.shape[-1]))


def body(
    sizes,
    q_hbm,
    k_hbm,
    v_hbm,
    w_hbm,
    lam_hbm,
    res_hbm,
    skip_hbm,
    gain_hbm,
    mix_ref,
    sum_ref,
    raw,
    w_ref,
    lam_ref,
    res_ref,
    skip_ref,
    gain_ref,
    halo,
    u_ref,
    qs_ref,
    y_ref,
    mix_s,
    kept,
    out_pow,
    scan_w,
    send_state,
    got_state,
    send_x,
    got_x,
    send_z,
    got_z,
    in_sem,
    par_sem,
    halo_s,
    halo_r,
    st_s,
    st_r,
    x_s,
    x_r,
    z_s,
    z_r,
    near_sem,
):
    n_ctx, n_chan, width, taps, modes = sizes
    rows = q_hbm.shape[0]
    steps = rows // SEG
    chunks = steps // CHUNK
    rim = taps - 1
    z_chips = n_chan // X_CHIPS
    ctx = lax.axis_index("ctx")
    chan = lax.axis_index("chan")
    my_x, my_z = lax.div(chan, z_chips), lax.rem(chan, z_chips)
    y_chips = n_ctx // 2
    my_y, my_core = lax.div(ctx, 2), lax.rem(ctx, 2)

    def along_ctx(k):
        return (lax.rem(ctx + k, n_ctx), chan)

    def along_y(k, core):
        return (2 * lax.rem(my_y + (k + y_chips), y_chips) + core, chan)

    def along_x(k):
        return (ctx, lax.rem(my_x + (k + X_CHIPS), X_CHIPS) * z_chips + my_z)

    def along_z(k):
        return (ctx, my_x * z_chips + lax.rem(my_z + (k + z_chips), z_chips))

    def all_of(got, *sems):
        part = got.at[pl.ds(1, got.shape[0] - 1)]
        for sem in sems:
            pltpu.make_async_copy(part, part, sem).wait()

    def tell(sem, *others):
        for other in others:
            pl.semaphore_signal(sem, inc=1, device_id=other, device_id_type=MESH)

    streams = (q_hbm, k_hbm, v_hbm)
    params = [
        pltpu.make_async_copy(src, dst, par_sem.at[i])
        for i, (src, dst) in enumerate(
            (
                (w_hbm, w_ref),
                (lam_hbm, lam_ref),
                (res_hbm, res_ref),
                (skip_hbm, skip_ref),
                (gain_hbm, gain_ref),
            )
        )
    ]
    loads = [pltpu.make_async_copy(streams[i], raw.at[i], in_sem.at[i]) for i in range(3)]
    loads[1].start()
    loads[2].start()
    for copy in params:
        copy.start()
    loads[0].start()

    barrier = pltpu.get_barrier_semaphore()
    tell(
        barrier,
        along_y(0, 1 - my_core),
        along_y(-1, 0),
        along_y(-1, 1),
        along_y(1, 0),
        along_y(1, 1),
        along_x(-1),
        along_x(1),
        along_z(-1),
        along_z(1),
    )
    for copy in params:
        copy.wait()

    lam = lam_ref[...]
    coef = res_ref[...] * jnp.sqrt(expm1_of_minus(2.0 * lam))
    decay = 1.0 - expm1_of_minus(lam)
    decay_b = per_mode(decay)

    segment = lax.broadcasted_iota(jnp.int32, (modes, SEG, width), 1)
    for i in range(3):
        weight = per_mode(jnp.exp(lam * (-1.0 * steps * 2**i)))
        scan_w[i] = jnp.where(segment >= 2**i, weight, 0.0)
    scan_w[3] = per_mode(jnp.exp(lam * (-1.0 * (steps - CHUNK))))

    def by_step(i, c):
        parts = [
            raw[i, pl.ds(pl.multiple_of(s * steps + c * CHUNK, CHUNK), CHUNK), :]
            for s in range(SEG)
        ]
        return jnp.swapaxes(jnp.stack(parts).astype(F32), 0, 1)

    def taps_of(i):
        return [in_all(w_ref[i, j : j + 1, :]) for j in range(taps)]

    def filtered(weights, window):
        total = weights[0][None] * window[rim:]
        for j in range(1, taps):
            total = total + weights[j][None] * window[rim - j : rim - j + CHUNK]
        return total

    def make_u(c, before_k, before_v):
        window_k = jnp.concatenate([before_k, by_step(1, c)], axis=0)
        window_v = jnp.concatenate([before_v, by_step(2, c)], axis=0)
        at = pl.ds(pl.multiple_of(c * CHUNK, CHUNK), CHUNK)
        u_ref[at] = filtered(w_k, window_k) * filtered(w_v, window_v)
        return window_k[CHUNK:], window_v[CHUNK:]

    def u_chunk(c, before):
        return make_u(c, *before)

    loads[1].wait()
    loads[2].wait()
    w_k, w_v = taps_of(1), taps_of(2)
    first_k, first_v = by_step(1, 0)[CHUNK - rim :], by_step(2, 0)[CHUNK - rim :]

    pl.semaphore_wait(barrier, 9)
    halos = [
        pltpu.make_async_remote_copy(
            src_ref=streams[i].at[pl.ds(rows - HALO, HALO)],
            dst_ref=halo.at[i],
            send_sem=halo_s.at[i],
            recv_sem=halo_r.at[i],
            device_id=along_ctx(1),
            device_id_type=MESH,
        )
        for i in range(3)
    ]
    for copy in halos:
        copy.start()
    tell(near_sem.at[0], along_y(-1, my_core), along_y(1, my_core))
    tell(near_sem.at[1], along_x(-1), along_x(1))
    tell(near_sem.at[2], along_z(-1), along_z(1))
    before = lax.fori_loop(1, chunks // 2, u_chunk, (first_k, first_v))

    for i in range(3):
        pl.semaphore_wait(near_sem.at[i], 2)
    tell(near_sem.at[3], along_y(-2, my_core), along_y(2, my_core))
    tell(near_sem.at[4], along_z(-2), along_z(2))
    tail_k, tail_v = lax.fori_loop(chunks // 2, chunks, u_chunk, before)

    def advance(c, state):
        for t in range(CHUNK):
            at = c * CHUNK + t
            if t % KEPT == 0:
                kept[c * (CHUNK // KEPT) + t // KEPT] = state
            state = decay_b * state + u_ref[at][None]
        return state

    zero_state = jnp.zeros((modes, SEG, width), F32)
    ends = lax.fori_loop(1, chunks, advance, zero_state)

    for copy in halos:
        copy.wait()
    has_before = (ctx > 0).astype(F32)
    top = lax.broadcasted_iota(jnp.int32, (rim, SEG, width), 1) == 0

    def entering(i, tail):
        rows_before = halo[i].astype(F32)[HALO - rim :] * has_before
        spread = jnp.broadcast_to(rows_before[:, None, :], (rim, SEG, width))
        return jnp.where(top, spread, pltpu.roll(tail, 1, 1))

    make_u(0, entering(1, tail_k), entering(2, tail_v))
    first = advance(0, zero_state)
    total = ends + scan_w[3] * first
    for i in range(3):
        total = total + scan_w[i] * pltpu.roll(total, 2**i, 1)
    send_state[...] = total[:, SEG - 1, :].astype(BF16)
    start = jnp.where(segment >= 1, pltpu.roll(total, 1, 1), 0.0)

    states = [
        pltpu.make_async_remote_copy(
            src_ref=send_state,
            dst_ref=got_state.at[k],
            send_sem=st_s.at[k],
            recv_sem=st_r.at[k],
            device_id=along_ctx(k),
            device_id_type=MESH,
        )
        for k in range(1, n_ctx)
    ]
    pl.semaphore_wait(near_sem.at[3], 2)
    for k in sorted(range(1, n_ctx), key=lambda k: abs(k - n_ctx // 2)):
        pl.when(ctx < n_ctx - k)(states[k - 1].start)
    pl.semaphore_wait(near_sem.at[4], 2)
    tell(near_sem.at[5], along_z(-4), along_z(4))

    loads[0].wait()
    w_q = taps_of(0)

    def q_chunk(c, before_q):
        window = jnp.concatenate([before_q, by_step(0, c)], axis=0)
        at = pl.ds(pl.multiple_of(c * CHUNK, CHUNK), CHUNK)
        qs_ref[at] = filtered(w_q, window)
        return window[CHUNK:]

    tail_q = by_step(0, chunks - 1)[CHUNK - rim :]
    lax.fori_loop(0, chunks, q_chunk, entering(0, tail_q))

    response = []
    power_of = coef
    for i in range(KEPT):
        response.append(in_all(jnp.sum(power_of, axis=0, keepdims=True)))
        power_of = power_of * decay
        out_pow[i] = per_mode(power_of)
    response[0] = response[0] + in_all(skip_ref[...])

    def y_chunk(c, carry):
        for b in range(CHUNK // KEPT):
            state = kept[c * (CHUNK // KEPT) + b]
            for i in range(KEPT):
                at = c * CHUNK + b * KEPT + i
                y = over_modes(out_pow[i] * state)
                for j in range(i + 1):
                    y = y + response[j] * u_ref[at - j]
                y_ref[at] = y
        return carry

    lax.fori_loop(0, chunks, y_chunk, 0)

    device_decay = jnp.exp(lam * (-1.0 * rows))
    lead = jnp.exp(per_mode(lam) * (-1.0 * steps * segment.astype(F32)))
    for k in range(1, n_ctx):
        pl.when(ctx < n_ctx - k)(states[k - 1].wait_send)
        pl.when(ctx >= k)(states[k - 1].wait_recv)
    incoming = jnp.zeros((modes, width), F32)
    for k in range(n_ctx - 1, 0, -1):
        got = jnp.where(ctx >= k, got_state[k].astype(F32), 0.0)
        incoming = device_decay * incoming + got

    lane = lax.broadcasted_iota(jnp.int32, (SEG, LANES), 1)
    gain = in_all(gain_ref[...])

    half = chunks // 2

    def with_power_of(c, power, base):
        place = lane - (c - base) * CHUNK
        for t in range(CHUNK):
            mixed = mix_s[c * CHUNK + t]
            power = jnp.where(
                place == t, jnp.sum(mixed * mixed, axis=1, keepdims=True), power
            )
        return power

    def mix_chunk(c, far):
        for t in range(CHUNK):
            at = c * CHUNK + t
            y = y_ref[at] + over_modes(out_pow[t % KEPT] * far)
            mix_s[at] = qs_ref[at] * y
            if t % KEPT == KEPT - 1:
                far = decay_kept * far
        return far

    def mix_and_power(c, carry, base):
        far, power = carry
        power = with_power_of(c - 1, power, base)
        return mix_chunk(c, far), power

    decay_kept = per_mode((decay * decay) * (decay * decay))
    no_power = jnp.zeros((SEG, LANES), F32)
    far = mix_chunk(0, start + lead * per_mode(incoming)) + first
    far, power_0 = lax.fori_loop(
        1, half + 1, functools.partial(mix_and_power, base=0), (far, no_power)
    )
    _, power_1 = lax.fori_loop(
        half + 1, chunks, functools.partial(mix_and_power, base=half), (far, no_power)
    )
    power_1 = with_power_of(chunks - 1, power_1, half)

    own = jnp.concatenate([power_0, power_1], axis=0)
    send_x[...] = own.astype(BF16)
    over_x = [
        pltpu.make_async_remote_copy(
            src_ref=send_x,
            dst_ref=got_x.at[k],
            send_sem=x_s,
            recv_sem=x_r,
            device_id=along_x(k),
            device_id_type=MESH,
        )
        for k in range(1, X_CHIPS)
    ]
    for copy in over_x:
        copy.start()

    def relayout(c, carry):
        at = pl.ds(pl.multiple_of(c * CHUNK, CHUNK), CHUNK)
        by_segment = jnp.swapaxes(mix_s[at] * gain, 0, 1)
        for s in range(SEG):
            to = pl.multiple_of(s * steps + c * CHUNK, CHUNK)
            mix_ref[pl.ds(to, CHUNK), :] = by_segment[s]
        return carry

    lax.fori_loop(0, chunks, relayout, 0)
    all_of(got_x, x_s, x_r)
    own = own + sum(got_x[k].astype(F32) for k in range(1, X_CHIPS))
    send_z[...] = own.astype(BF16)
    over_z = [
        pltpu.make_async_remote_copy(
            src_ref=send_z,
            dst_ref=got_z.at[k],
            send_sem=z_s,
            recv_sem=z_r,
            device_id=along_z(k),
            device_id_type=MESH,
        )
        for k in range(1, z_chips)
    ]
    pl.semaphore_wait(near_sem.at[5], 2)
    for copy in over_z:
        copy.start()
    all_of(got_z, z_s, z_r)
    sum_ref[...] = own + sum(got_z[k].astype(F32) for k in range(1, z_chips))


def finish(channels, mix_ref, sum_ref, out_hbm, out_v, out_sem):
    groups = sum_ref.shape[0]
    scale = lax.rsqrt(sum_ref[...] * (1.0 / channels) + 1e-05)
    halves = groups // SEG
    outs = []
    for g in range(groups):
        row = (g % halves) * SEG + g // halves
        spread = jnp.broadcast_to(scale[row : row + 1], (LANES, LANES)).T
        at = pl.ds(g * LANES, LANES)
        out_v[at, :] = (mix_ref[at, :] * spread).astype(BF16)
        if g % 4 == 3:
            span = pl.ds((g - 3) * LANES, 4 * LANES)
            copy = pltpu.make_async_copy(out_v.at[span], out_hbm.at[span], out_sem.at[g // 4])
            copy.start()
            outs.append(copy)
    for copy in outs:
        copy.wait()


def shards(n_ctx, n_chan, queries, keys_in, values_in, short_weights, decay_rates, residues, skip_term, out_gain):
    rows, width = queries.shape[1:]
    taps, modes = short_weights.shape[1], decay_rates.shape[0]
    steps, groups = rows // SEG, rows // LANES
    z_chips = n_chan // X_CHIPS
    dma = pltpu.SemaphoreType.DMA
    vmem = pl.BlockSpec(memory_space=pltpu.VMEM)
    hbm = pl.BlockSpec(memory_space=pltpu.HBM)
    mixed, sums = pl.pallas_call(
        functools.partial(body, (n_ctx, n_chan, width, taps, modes)),
        out_shape=(
            jax.ShapeDtypeStruct((rows, width), F32),
            jax.ShapeDtypeStruct((groups, LANES), F32),
        ),
        in_specs=[hbm] * 8,
        out_specs=(vmem, vmem),
        scratch_shapes=[
            pltpu.VMEM((3, rows, width), BF16),
            pltpu.VMEM((3, taps, width), F32),
            pltpu.VMEM((modes, width), F32),
            pltpu.VMEM((modes, width), F32),
            pltpu.VMEM((1, width), F32),
            pltpu.VMEM((1, width), F32),
            pltpu.VMEM((3, HALO, width), BF16),
            pltpu.VMEM((steps, SEG, width), F32),
            pltpu.VMEM((steps, SEG, width), F32),
            pltpu.VMEM((steps, SEG, width), F32),
            pltpu.VMEM((steps, SEG, width), F32),
            pltpu.VMEM((steps // KEPT, modes, SEG, width), F32),
            pltpu.VMEM((KEPT, modes, SEG, width), F32),
            pltpu.VMEM((4, modes, SEG, width), F32),
            pltpu.VMEM((modes, width), BF16),
            pltpu.VMEM((n_ctx, modes, width), BF16),
            pltpu.VMEM((groups, LANES), BF16),
            pltpu.VMEM((X_CHIPS, groups, LANES), BF16),
            pltpu.VMEM((groups, LANES), BF16),
            pltpu.VMEM((z_chips, groups, LANES), BF16),
            dma((3,)),
            dma((5,)),
            dma((3,)),
            dma((3,)),
            dma((n_ctx,)),
            dma((n_ctx,)),
            dma,
            dma,
            dma,
            dma,
            pltpu.SemaphoreType.REGULAR((6,)),
        ],
        compiler_params=pltpu.CompilerParams(
            collective_id=0, has_side_effects=True, vmem_limit_bytes=24 << 20
        ),
        name="hyena",
    )(
        *(
            pltpu.with_memory_space_constraint(x, pltpu.HBM)
            for x in (
                queries[0],
                keys_in[0],
                values_in[0],
                short_weights,
                decay_rates,
                residues,
                skip_term[None],
                out_gain[None],
            )
        )
    )
    out = pl.pallas_call(
        functools.partial(finish, width * n_chan),
        out_shape=jax.ShapeDtypeStruct((rows, width), BF16),
        in_specs=[vmem, vmem],
        out_specs=hbm,
        scratch_shapes=[pltpu.VMEM((rows, width), BF16), dma((groups // 4,))],
        compiler_params=pltpu.CompilerParams(vmem_limit_bytes=8 << 20),
        name="finish",
    )(mixed, sums)
    return out[None]


def solution(mesh):
    placed = (
        P(None, "ctx", "chan"),
        P(None, "ctx", "chan"),
        P(None, "ctx", "chan"),
        P(None, None, "chan"),
        P(None, "chan"),
        P(None, "chan"),
        P("chan"),
        P("chan"),
    )
    return jax.shard_map(
        functools.partial(shards, mesh.shape["ctx"], mesh.shape["chan"]),
        mesh=mesh,
        in_specs=placed,
        out_specs=P(None, "ctx", "chan"),
        check_vma=False,
    )
```

```python
import functools

import jax
import jax.numpy as jnp
from jax import lax
from jax.experimental import pallas as pl
from jax.experimental.pallas import tpu as pltpu
from jax.sharding import PartitionSpec as P

MESH = pl.DeviceIdType.MESH
F32 = jnp.float32
BF16 = jnp.bfloat16
SEG = 8
LANES = 128
CHUNK = 16
KEPT = 4
HALO = 16
X_CHIPS = 4


def expm1_of_minus(x):
    series = jnp.full_like(x, 1.0 / 40320.0)
    for factor in (5040.0, 720.0, 120.0, 24.0, 6.0, 2.0, 1.0):
        series = 1.0 / factor - x * series
    return jnp.where(x < 0.25, x * series, 1.0 - jnp.exp(-x))


def per_mode(rows):
    return jnp.broadcast_to(rows[:, None, :], (rows.shape[0], SEG, rows.shape[1]))


def over_modes(terms):
    while terms.shape[0] > 1:
        half = terms.shape[0] // 2
        terms = terms[:half] + terms[half:]
    return terms[0]


def in_all(row):
    return jnp.broadcast_to(row, (SEG, row.shape[-1]))


def body(
    sizes,
    q_hbm,
    k_hbm,
    v_hbm,
    w_hbm,
    lam_hbm,
    res_hbm,
    skip_hbm,
    gain_hbm,
    mix_ref,
    sum_ref,
    raw,
    w_ref,
    lam_ref,
    res_ref,
    skip_ref,
    gain_ref,
    halo,
    u_ref,
    qs_ref,
    y_ref,
    mix_s,
    kept,
    out_pow,
    scan_w,
    send_state,
    got_state,
    send_x,
    got_x,
    send_z,
    got_z,
    in_sem,
    par_sem,
    halo_s,
    halo_r,
    st_s,
    st_r,
    x_s,
    x_r,
    z_s,
    z_r,
    near_sem,
):
    n_ctx, n_chan, width, taps, modes = sizes
    rows = q_hbm.shape[0]
    steps = rows // SEG
    chunks = steps // CHUNK
    rim = taps - 1
    z_chips = n_chan // X_CHIPS
    ctx = lax.axis_index("ctx")
    chan = lax.axis_index("chan")
    my_x, my_z = lax.div(chan, z_chips), lax.rem(chan, z_chips)
    y_chips = n_ctx // 2
    my_y, my_core = lax.div(ctx, 2), lax.rem(ctx, 2)

    def along_ctx(k):
        return (lax.rem(ctx + k, n_ctx), chan)

    def along_y(k, core):
        return (2 * lax.rem(my_y + (k + y_chips), y_chips) + core, chan)

    def along_x(k):
        return (ctx, lax.rem(my_x + (k + X_CHIPS), X_CHIPS) * z_chips + my_z)

    def along_z(k):
        return (ctx, my_x * z_chips + lax.rem(my_z + (k + z_chips), z_chips))

    def all_of(got, *sems):
        part = got.at[pl.ds(1, got.shape[0] - 1)]
        for sem in sems:
            pltpu.make_async_copy(part, part, sem).wait()

    def tell(sem, *others):
        for other in others:
            pl.semaphore_signal(sem, inc=1, device_id=other, device_id_type=MESH)

    streams = (q_hbm, k_hbm, v_hbm)
    params = [
        pltpu.make_async_copy(src, dst, par_sem.at[i])
        for i, (src, dst) in enumerate(
            (
                (w_hbm, w_ref),
                (lam_hbm, lam_ref),
                (res_hbm, res_ref),
                (skip_hbm, skip_ref),
                (gain_hbm, gain_ref),
            )
        )
    ]
    loads = [pltpu.make_async_copy(streams[i], raw.at[i], in_sem.at[i]) for i in range(3)]
    loads[1].start()
    loads[2].start()
    for copy in params:
        copy.start()
    loads[0].start()

    barrier = pltpu.get_barrier_semaphore()
    tell(
        barrier,
        along_y(0, 1 - my_core),
        along_y(-1, 0),
        along_y(-1, 1),
        along_y(1, 0),
        along_y(1, 1),
        along_x(-1),
        along_x(1),
        along_z(-1),
        along_z(1),
    )
    for copy in params:
        copy.wait()

    lam = lam_ref[...]
    coef = res_ref[...] * jnp.sqrt(expm1_of_minus(2.0 * lam))
    decay = 1.0 - expm1_of_minus(lam)
    decay_b = per_mode(decay)

    segment = lax.broadcasted_iota(jnp.int32, (modes, SEG, width), 1)
    for i in range(3):
        weight = per_mode(jnp.exp(lam * (-1.0 * steps * 2**i)))
        scan_w[i] = jnp.where(segment >= 2**i, weight, 0.0)
    scan_w[3] = per_mode(jnp.exp(lam * (-1.0 * (steps - CHUNK))))

    def by_step(i, c):
        parts = [
            raw[i, pl.ds(pl.multiple_of(s * steps + c * CHUNK, CHUNK), CHUNK), :]
            for s in range(SEG)
        ]
        return jnp.swapaxes(jnp.stack(parts).astype(F32), 0, 1)

    def taps_of(i):
        return [in_all(w_ref[i, j : j + 1, :]) for j in range(taps)]

    def filtered(weights, window):
        total = weights[0][None] * window[rim:]
        for j in range(1, taps):
            total = total + weights[j][None] * window[rim - j : rim - j + CHUNK]
        return total

    def make_u(c, before_k, before_v):
        window_k = jnp.concatenate([before_k, by_step(1, c)], axis=0)
        window_v = jnp.concatenate([before_v, by_step(2, c)], axis=0)
        at = pl.ds(pl.multiple_of(c * CHUNK, CHUNK), CHUNK)
        u_ref[at] = filtered(w_k, window_k) * filtered(w_v, window_v)
        return window_k[CHUNK:], window_v[CHUNK:]

    def u_chunk(c, before):
        return make_u(c, *before)

    loads[1].wait()
    loads[2].wait()
    w_k, w_v = taps_of(1), taps_of(2)
    first_k, first_v = by_step(1, 0)[CHUNK - rim :], by_step(2, 0)[CHUNK - rim :]

    pl.semaphore_wait(barrier, 9)
    halos = [
        pltpu.make_async_remote_copy(
            src_ref=streams[i].at[pl.ds(rows - HALO, HALO)],
            dst_ref=halo.at[i],
            send_sem=halo_s.at[i],
            recv_sem=halo_r.at[i],
            device_id=along_ctx(1),
            device_id_type=MESH,
        )
        for i in range(3)
    ]
    for copy in halos:
        copy.start()
    tell(near_sem.at[0], along_y(-1, my_core), along_y(1, my_core))
    tell(near_sem.at[1], along_x(-1), along_x(1))
    tell(near_sem.at[2], along_z(-1), along_z(1))
    before = lax.fori_loop(1, chunks // 2, u_chunk, (first_k, first_v))

    for i in range(3):
        pl.semaphore_wait(near_sem.at[i], 2)
    tell(near_sem.at[3], along_y(-2, my_core), along_y(2, my_core))
    tell(near_sem.at[4], along_z(-2), along_z(2))
    tail_k, tail_v = lax.fori_loop(chunks // 2, chunks, u_chunk, before)

    def advance(c, state):
        for t in range(CHUNK):
            at = c * CHUNK + t
            if t % KEPT == 0:
                kept[c * (CHUNK // KEPT) + t // KEPT] = state
            state = decay_b * state + u_ref[at][None]
        return state

    zero_state = jnp.zeros((modes, SEG, width), F32)
    ends = lax.fori_loop(1, chunks, advance, zero_state)

    for copy in halos:
        copy.wait()
    has_before = (ctx > 0).astype(F32)
    top = lax.broadcasted_iota(jnp.int32, (rim, SEG, width), 1) == 0

    def entering(i, tail):
        rows_before = halo[i].astype(F32)[HALO - rim :] * has_before
        spread = jnp.broadcast_to(rows_before[:, None, :], (rim, SEG, width))
        return jnp.where(top, spread, pltpu.roll(tail, 1, 1))

    make_u(0, entering(1, tail_k), entering(2, tail_v))
    first = advance(0, zero_state)
    total = ends + scan_w[3] * first
    for i in range(3):
        total = total + scan_w[i] * pltpu.roll(total, 2**i, 1)
    send_state[...] = total[:, SEG - 1, :].astype(BF16)
    start = jnp.where(segment >= 1, pltpu.roll(total, 1, 1), 0.0)

    states = [
        pltpu.make_async_remote_copy(
            src_ref=send_state,
            dst_ref=got_state.at[k],
            send_sem=st_s.at[k],
            recv_sem=st_r.at[k],
            device_id=along_ctx(k),
            device_id_type=MESH,
        )
        for k in range(1, n_ctx)
    ]
    pl.semaphore_wait(near_sem.at[3], 2)
    for k in sorted(range(1, n_ctx), key=lambda k: abs(k - n_ctx // 2)):
        pl.when(ctx < n_ctx - k)(states[k - 1].start)
    pl.semaphore_wait(near_sem.at[4], 2)
    tell(near_sem.at[5], along_z(-4), along_z(4))

    loads[0].wait()
    w_q = taps_of(0)

    def q_chunk(c, before_q):
        window = jnp.concatenate([before_q, by_step(0, c)], axis=0)
        at = pl.ds(pl.multiple_of(c * CHUNK, CHUNK), CHUNK)
        qs_ref[at] = filtered(w_q, window)
        return window[CHUNK:]

    tail_q = by_step(0, chunks - 1)[CHUNK - rim :]
    lax.fori_loop(0, chunks, q_chunk, entering(0, tail_q))

    response = []
    power_of = coef
    for i in range(CHUNK):
        if i < KEPT:
            response.append(in_all(jnp.sum(power_of, axis=0, keepdims=True)))
        power_of = power_of * decay
        out_pow[i] = per_mode(power_of)
    response[0] = response[0] + in_all(skip_ref[...])

    def y_chunk(c, carry):
        for b in range(CHUNK // KEPT):
            state = kept[c * (CHUNK // KEPT) + b]
            for i in range(KEPT):
                at = c * CHUNK + b * KEPT + i
                y = over_modes(out_pow[i] * state)
                for j in range(i + 1):
                    y = y + response[j] * u_ref[at - j]
                y_ref[at] = y
        return carry

    lax.fori_loop(0, chunks, y_chunk, 0)

    lead = jnp.exp(per_mode(lam) * (-1.0 * steps * segment.astype(F32)))
    decay_chunk = per_mode(jnp.exp(lam * (-1.0 * CHUNK)))
    reach = [
        jnp.where(ctx >= k, jnp.exp(lam * (-1.0 * rows * (k - 1))), 0.0)
        for k in range(1, n_ctx)
    ]
    for k in range(1, n_ctx):
        pl.when(ctx >= k)(states[k - 1].wait_recv)
    terms = [
        jnp.where(ctx >= k, got_state[k].astype(F32), 0.0) * reach[k - 1]
        for k in range(1, n_ctx)
    ]
    while len(terms) > 1:
        terms = [sum(terms[i : i + 2]) for i in range(0, len(terms), 2)]
    incoming = terms[0]

    lane = lax.broadcasted_iota(jnp.int32, (SEG, LANES), 1)
    gain = in_all(gain_ref[...])

    half = chunks // 2

    def with_power_of(c, power, base):
        place = lane - (c - base) * CHUNK
        for t in range(CHUNK):
            mixed = mix_s[(c + 1) * CHUNK + t]
            power = jnp.where(
                place == t, jnp.sum(mixed * mixed, axis=1, keepdims=True), power
            )
        return power

    def mix_chunk(c, far):
        for t in range(CHUNK):
            at = c * CHUNK + t
            y = y_ref[at] + over_modes(out_pow[t] * far)
            mix_s[at + CHUNK] = qs_ref[at] * y
        return decay_chunk * far

    def mix_pair(p, carry, base):
        far, power = carry
        power = with_power_of(2 * p - 1, power, base)
        far = mix_chunk(2 * p, far) + first * (p == 0).astype(F32)
        power = with_power_of(2 * p, power, base)
        return mix_chunk(2 * p + 1, far), power

    no_power = jnp.zeros((SEG, LANES), F32)
    mix_s[0:CHUNK] = jnp.zeros((CHUNK, SEG, width), F32)
    far = start + lead * per_mode(incoming)
    far, power_0 = lax.fori_loop(
        0, half // 2, functools.partial(mix_pair, base=0), (far, no_power)
    )
    power_0 = with_power_of(half - 1, power_0, 0)
    _, power_1 = lax.fori_loop(
        half // 2, half, functools.partial(mix_pair, base=half), (far, no_power)
    )
    power_1 = with_power_of(chunks - 1, power_1, half)

    own = jnp.concatenate([power_0, power_1], axis=0)
    send_x[...] = own.astype(BF16)
    over_x = [
        pltpu.make_async_remote_copy(
            src_ref=send_x,
            dst_ref=got_x.at[k],
            send_sem=x_s,
            recv_sem=x_r,
            device_id=along_x(k),
            device_id_type=MESH,
        )
        for k in range(1, X_CHIPS)
    ]
    for copy in over_x:
        copy.start()

    def relayout(c, carry):
        at = pl.ds(pl.multiple_of((c + 1) * CHUNK, CHUNK), CHUNK)
        by_segment = jnp.swapaxes(mix_s[at] * gain, 0, 1)
        for s in range(SEG):
            to = pl.multiple_of(s * steps + c * CHUNK, CHUNK)
            mix_ref[pl.ds(to, CHUNK), :] = by_segment[s]
        return carry

    lax.fori_loop(0, chunks, relayout, 0)
    for k in range(1, n_ctx):
        pl.when(ctx < n_ctx - k)(states[k - 1].wait_send)
    all_of(got_x, x_r)
    own = own + sum(got_x[k].astype(F32) for k in range(1, X_CHIPS))
    send_z[...] = own.astype(BF16)
    over_z = [
        pltpu.make_async_remote_copy(
            src_ref=send_z,
            dst_ref=got_z.at[k],
            send_sem=z_s,
            recv_sem=z_r,
            device_id=along_z(k),
            device_id_type=MESH,
        )
        for k in range(1, z_chips)
    ]
    pl.semaphore_wait(near_sem.at[5], 2)
    for copy in over_z:
        copy.start()
    all_of(got_x, x_s)
    all_of(got_z, z_s)
    all_of(got_z, z_r)
    terms = [own] + [got_z[k].astype(F32) for k in range(1, z_chips)]
    while len(terms) > 1:
        terms = [sum(terms[i : i + 2]) for i in range(0, len(terms), 2)]
    sum_ref[...] = terms[0]


def finish(channels, mix_ref, sum_ref, out_hbm, out_v, out_sem):
    groups = sum_ref.shape[0]
    scale = lax.rsqrt(sum_ref[...] * (1.0 / channels) + 1e-05)
    high = scale.astype(BF16).astype(F32)
    middle = (scale - high).astype(BF16).astype(F32)
    low = scale - high - middle
    unused = jnp.zeros((LANES - 3 * groups, LANES), F32)
    columns = jnp.concatenate([high, middle, low, unused], axis=0).T.astype(BF16)
    lane = lax.broadcasted_iota(jnp.int32, (LANES, LANES), 1)
    group_of = jnp.where(lane < 3 * groups, lane % groups, groups)
    ones = jnp.ones((LANES, LANES), BF16)
    halves = groups // SEG
    outs = []
    for g in range(groups):
        row = (g % halves) * SEG + g // halves
        if g % 2 == 0:
            picked = jnp.where(group_of == row, columns, jnp.zeros_like(columns))
            spread = jnp.dot(picked, ones, preferred_element_type=F32)
        else:
            spread = jnp.broadcast_to(scale[row : row + 1], (LANES, LANES)).T
        at = pl.ds(g * LANES, LANES)
        out_v[at, :] = (mix_ref[at, :] * spread).astype(BF16)
        if g % 4 == 3:
            span = pl.ds((g - 3) * LANES, 4 * LANES)
            copy = pltpu.make_async_copy(out_v.at[span], out_hbm.at[span], out_sem.at[g // 4])
            copy.start()
            outs.append(copy)
    for copy in outs:
        copy.wait()


def shards(n_ctx, n_chan, queries, keys_in, values_in, short_weights, decay_rates, residues, skip_term, out_gain):
    rows, width = queries.shape[1:]
    taps, modes = short_weights.shape[1], decay_rates.shape[0]
    steps, groups = rows // SEG, rows // LANES
    z_chips = n_chan // X_CHIPS
    dma = pltpu.SemaphoreType.DMA
    vmem = pl.BlockSpec(memory_space=pltpu.VMEM)
    hbm = pl.BlockSpec(memory_space=pltpu.HBM)
    mixed, sums = pl.pallas_call(
        functools.partial(body, (n_ctx, n_chan, width, taps, modes)),
        out_shape=(
            jax.ShapeDtypeStruct((rows, width), F32),
            jax.ShapeDtypeStruct((groups, LANES), F32),
        ),
        in_specs=[hbm] * 8,
        out_specs=(vmem, vmem),
        scratch_shapes=[
            pltpu.VMEM((3, rows, width), BF16),
            pltpu.VMEM((3, taps, width), F32),
            pltpu.VMEM((modes, width), F32),
            pltpu.VMEM((modes, width), F32),
            pltpu.VMEM((1, width), F32),
            pltpu.VMEM((1, width), F32),
            pltpu.VMEM((3, HALO, width), BF16),
            pltpu.VMEM((steps, SEG, width), F32),
            pltpu.VMEM((steps, SEG, width), F32),
            pltpu.VMEM((steps, SEG, width), F32),
            pltpu.VMEM((steps + CHUNK, SEG, width), F32),
            pltpu.VMEM((steps // KEPT, modes, SEG, width), F32),
            pltpu.VMEM((CHUNK, modes, SEG, width), F32),
            pltpu.VMEM((4, modes, SEG, width), F32),
            pltpu.VMEM((modes, width), BF16),
            pltpu.VMEM((n_ctx, modes, width), BF16),
            pltpu.VMEM((groups, LANES), BF16),
            pltpu.VMEM((X_CHIPS, groups, LANES), BF16),
            pltpu.VMEM((groups, LANES), BF16),
            pltpu.VMEM((z_chips, groups, LANES), BF16),
            dma((3,)),
            dma((5,)),
            dma((3,)),
            dma((3,)),
            dma((n_ctx,)),
            dma((n_ctx,)),
            dma,
            dma,
            dma,
            dma,
            pltpu.SemaphoreType.REGULAR((6,)),
        ],
        compiler_params=pltpu.CompilerParams(
            collective_id=0, has_side_effects=True, vmem_limit_bytes=24 << 20
        ),
        name="hyena",
    )(
        *(
            pltpu.with_memory_space_constraint(x, pltpu.HBM)
            for x in (
                queries[0],
                keys_in[0],
                values_in[0],
                short_weights,
                decay_rates,
                residues,
                skip_term[None],
                out_gain[None],
            )
        )
    )
    out = pl.pallas_call(
        functools.partial(finish, width * n_chan),
        out_shape=jax.ShapeDtypeStruct((rows, width), BF16),
        in_specs=[vmem, vmem],
        out_specs=hbm,
        scratch_shapes=[pltpu.VMEM((rows, width), BF16), dma((groups // 4,))],
        compiler_params=pltpu.CompilerParams(vmem_limit_bytes=8 << 20),
        name="finish",
    )(mixed, sums)
    return out[None]


def solution(mesh):
    placed = (
        P(None, "ctx", "chan"),
        P(None, "ctx", "chan"),
        P(None, "ctx", "chan"),
        P(None, None, "chan"),
        P(None, "chan"),
        P(None, "chan"),
        P("chan"),
        P("chan"),
    )
    return jax.shard_map(
        functools.partial(shards, mesh.shape["ctx"], mesh.shape["chan"]),
        mesh=mesh,
        in_specs=placed,
        out_specs=P(None, "ctx", "chan"),
        check_vma=False,
    )
```

```python
import functools

import jax
import jax.numpy as jnp
from jax import lax
from jax.experimental import pallas as pl
from jax.experimental.pallas import tpu as pltpu
from jax.sharding import PartitionSpec as P

MESH = pl.DeviceIdType.MESH
F32 = jnp.float32
BF16 = jnp.bfloat16
SEG = 8
LANES = 128
CHUNK = 16
KEPT = 4
HALO = 16
X_CHIPS = 4


def expm1_of_minus(x):
    series = jnp.full_like(x, 1.0 / 40320.0)
    for factor in (5040.0, 720.0, 120.0, 24.0, 6.0, 2.0, 1.0):
        series = 1.0 / factor - x * series
    return jnp.where(x < 0.25, x * series, 1.0 - jnp.exp(-x))


def per_mode(rows):
    return jnp.broadcast_to(rows[:, None, :], (rows.shape[0], SEG, rows.shape[1]))


def over_modes(terms):
    while terms.shape[0] > 1:
        half = terms.shape[0] // 2
        terms = terms[:half] + terms[half:]
    return terms[0]


def in_all(row):
    return jnp.broadcast_to(row, (SEG, row.shape[-1]))


def body(
    sizes,
    q_hbm,
    k_hbm,
    v_hbm,
    w_hbm,
    lam_hbm,
    res_hbm,
    skip_hbm,
    gain_hbm,
    mix_ref,
    sum_ref,
    raw,
    w_ref,
    lam_ref,
    res_ref,
    skip_ref,
    gain_ref,
    halo,
    u_ref,
    qs_ref,
    y_ref,
    mix_s,
    kept,
    out_pow,
    scan_w,
    send_state,
    got_state,
    send_x,
    got_x,
    send_z,
    got_z,
    in_sem,
    par_sem,
    halo_s,
    halo_r,
    st_s,
    st_r,
    x_s,
    x_r,
    z_s,
    z_r,
    near_sem,
):
    n_ctx, n_chan, width, taps, modes = sizes
    steps = q_hbm.shape[1]
    rows = SEG * steps
    chunks = steps // CHUNK
    rim = taps - 1
    z_chips = n_chan // X_CHIPS
    ctx = lax.axis_index("ctx")
    chan = lax.axis_index("chan")
    my_x, my_z = lax.div(chan, z_chips), lax.rem(chan, z_chips)
    y_chips = n_ctx // 2
    my_y, my_core = lax.div(ctx, 2), lax.rem(ctx, 2)

    def along_ctx(k):
        return (lax.rem(ctx + k, n_ctx), chan)

    def along_y(k, core):
        return (2 * lax.rem(my_y + (k + y_chips), y_chips) + core, chan)

    def along_x(k):
        return (ctx, lax.rem(my_x + (k + X_CHIPS), X_CHIPS) * z_chips + my_z)

    def along_z(k):
        return (ctx, my_x * z_chips + lax.rem(my_z + (k + z_chips), z_chips))

    def all_of(got, *sems):
        part = got.at[pl.ds(1, got.shape[0] - 1)]
        for sem in sems:
            pltpu.make_async_copy(part, part, sem).wait()

    def tell(sem, *others):
        for other in others:
            pl.semaphore_signal(sem, inc=1, device_id=other, device_id_type=MESH)

    streams = (q_hbm, k_hbm, v_hbm)
    params = [
        pltpu.make_async_copy(src, dst, par_sem.at[i])
        for i, (src, dst) in enumerate(
            (
                (w_hbm, w_ref),
                (lam_hbm, lam_ref),
                (res_hbm, res_ref),
                (skip_hbm, skip_ref),
                (gain_hbm, gain_ref),
            )
        )
    ]
    loads = [
        [
            pltpu.make_async_copy(
                streams[i].at[:, pl.ds(h * (steps // 2), steps // 2)],
                raw.at[i, :, pl.ds(h * (steps // 2), steps // 2)],
                in_sem.at[i, h],
            )
            for h in range(2)
        ]
        for i in range(3)
    ]
    for copy in params:
        copy.start()
    for h in range(2):
        loads[1][h].start()
        loads[2][h].start()
    for h in range(2):
        loads[0][h].start()

    barrier = pltpu.get_barrier_semaphore()
    tell(
        barrier,
        along_y(0, 1 - my_core),
        along_y(-1, 0),
        along_y(-1, 1),
        along_y(1, 0),
        along_y(1, 1),
        along_x(-1),
        along_x(1),
        along_z(-1),
        along_z(1),
    )
    for copy in params:
        copy.wait()

    lam = lam_ref[...]
    coef = res_ref[...] * jnp.sqrt(expm1_of_minus(2.0 * lam))
    decay = 1.0 - expm1_of_minus(lam)
    decay_b = per_mode(decay)

    segment = lax.broadcasted_iota(jnp.int32, (modes, SEG, width), 1)
    for i in range(3):
        weight = per_mode(jnp.exp(lam * (-1.0 * steps * 2**i)))
        scan_w[i] = jnp.where(segment >= 2**i, weight, 0.0)
    scan_w[3] = per_mode(jnp.exp(lam * (-1.0 * (steps - CHUNK))))

    def by_step(i, c):
        part = raw[i, :, pl.ds(pl.multiple_of(c * CHUNK, CHUNK), CHUNK), :]
        return jnp.swapaxes(part.astype(F32), 0, 1)

    def taps_of(i):
        return [in_all(w_ref[i, j : j + 1, :]) for j in range(taps)]

    def filtered(weights, window):
        total = weights[0][None] * window[rim:]
        for j in range(1, taps):
            total = total + weights[j][None] * window[rim - j : rim - j + CHUNK]
        return total

    def make_u(c, before_k, before_v):
        window_k = jnp.concatenate([before_k, by_step(1, c)], axis=0)
        window_v = jnp.concatenate([before_v, by_step(2, c)], axis=0)
        at = pl.ds(pl.multiple_of(c * CHUNK, CHUNK), CHUNK)
        u_ref[at] = filtered(w_k, window_k) * filtered(w_v, window_v)
        return window_k[CHUNK:], window_v[CHUNK:]

    def u_chunk(c, before):
        return make_u(c, *before)

    for i in (1, 2):
        loads[i][0].wait()
    w_k, w_v = taps_of(1), taps_of(2)
    first_k, first_v = by_step(1, 0)[CHUNK - rim :], by_step(2, 0)[CHUNK - rim :]

    pl.semaphore_wait(barrier, 9)
    halos = [
        pltpu.make_async_remote_copy(
            src_ref=streams[i].at[SEG - 1, pl.ds(steps - HALO, HALO)],
            dst_ref=halo.at[i],
            send_sem=halo_s.at[i],
            recv_sem=halo_r.at[i],
            device_id=along_ctx(1),
            device_id_type=MESH,
        )
        for i in range(3)
    ]
    for copy in halos:
        copy.start()
    tell(near_sem.at[0], along_y(-1, my_core), along_y(1, my_core))
    tell(near_sem.at[1], along_x(-1), along_x(1))
    tell(near_sem.at[2], along_z(-1), along_z(1))
    before = lax.fori_loop(1, chunks // 2, u_chunk, (first_k, first_v))

    for i in (1, 2):
        loads[i][1].wait()
    tail_k, tail_v = lax.fori_loop(chunks // 2, chunks, u_chunk, before)

    pl.semaphore_wait(near_sem.at[0], 2)
    tell(near_sem.at[3], along_y(-2, my_core), along_y(2, my_core))

    def advance(c, state):
        for t in range(CHUNK):
            at = c * CHUNK + t
            if t % KEPT == 0:
                kept[c * (CHUNK // KEPT) + t // KEPT] = state
            state = decay_b * state + u_ref[at][None]
        return state

    zero_state = jnp.zeros((modes, SEG, width), F32)
    ends = lax.fori_loop(1, chunks, advance, zero_state)

    pl.semaphore_wait(near_sem.at[1], 2)
    pl.semaphore_wait(near_sem.at[2], 2)
    tell(near_sem.at[4], along_z(-2), along_z(2))
    for copy in halos:
        copy.wait()
    has_before = (ctx > 0).astype(F32)
    top = lax.broadcasted_iota(jnp.int32, (rim, SEG, width), 1) == 0

    def entering(i, tail):
        rows_before = halo[i].astype(F32)[HALO - rim :] * has_before
        spread = jnp.broadcast_to(rows_before[:, None, :], (rim, SEG, width))
        return jnp.where(top, spread, pltpu.roll(tail, 1, 1))

    make_u(0, entering(1, tail_k), entering(2, tail_v))
    first = advance(0, zero_state)
    total = ends + scan_w[3] * first
    for i in range(3):
        total = total + scan_w[i] * pltpu.roll(total, 2**i, 1)
    send_state[...] = total[:, SEG - 1, :].astype(BF16)
    start = jnp.where(segment >= 1, pltpu.roll(total, 1, 1), 0.0)

    states = [
        pltpu.make_async_remote_copy(
            src_ref=send_state,
            dst_ref=got_state.at[k],
            send_sem=st_s.at[k],
            recv_sem=st_r.at[k],
            device_id=along_ctx(k),
            device_id_type=MESH,
        )
        for k in range(1, n_ctx)
    ]
    pl.semaphore_wait(near_sem.at[3], 2)
    for k in sorted(range(1, n_ctx), key=lambda k: abs(k - n_ctx // 2)):
        pl.when(ctx < n_ctx - k)(states[k - 1].start)

    for copy in loads[0]:
        copy.wait()
    w_q = taps_of(0)

    def q_chunk(c, before_q):
        window = jnp.concatenate([before_q, by_step(0, c)], axis=0)
        at = pl.ds(pl.multiple_of(c * CHUNK, CHUNK), CHUNK)
        qs_ref[at] = filtered(w_q, window)
        return window[CHUNK:]

    tail_q = by_step(0, chunks - 1)[CHUNK - rim :]
    lax.fori_loop(0, chunks, q_chunk, entering(0, tail_q))

    pl.semaphore_wait(near_sem.at[4], 2)
    tell(near_sem.at[5], along_z(-4), along_z(4))

    response = []
    power_of = coef
    for i in range(CHUNK):
        if i < KEPT:
            response.append(in_all(jnp.sum(power_of, axis=0, keepdims=True)))
        power_of = power_of * decay
        out_pow[i] = per_mode(power_of)
    response[0] = response[0] + in_all(skip_ref[...])

    def y_chunk(c, carry):
        for b in range(CHUNK // KEPT):
            state = kept[c * (CHUNK // KEPT) + b]
            for i in range(KEPT):
                at = c * CHUNK + b * KEPT + i
                y = over_modes(out_pow[i] * state)
                for j in range(i + 1):
                    y = y + response[j] * u_ref[at - j]
                y_ref[at] = y
        return carry

    lax.fori_loop(0, chunks, y_chunk, 0)

    lead = jnp.exp(per_mode(lam) * (-1.0 * steps * segment.astype(F32)))
    decay_chunk = per_mode(jnp.exp(lam * (-1.0 * CHUNK)))
    reach = [
        jnp.where(ctx >= k, jnp.exp(lam * (-1.0 * rows * (k - 1))), 0.0)
        for k in range(1, n_ctx)
    ]
    for k in range(1, n_ctx):
        pl.when(ctx >= k)(states[k - 1].wait_recv)
    terms = [
        jnp.where(ctx >= k, got_state[k].astype(F32), 0.0) * reach[k - 1]
        for k in range(1, n_ctx)
    ]
    while len(terms) > 1:
        terms = [sum(terms[i : i + 2]) for i in range(0, len(terms), 2)]
    incoming = terms[0]

    lane = lax.broadcasted_iota(jnp.int32, (SEG, LANES), 1)
    gain = in_all(gain_ref[...])

    half = chunks // 2

    def with_power_of(c, power, base):
        place = lane - (c - base) * CHUNK
        for t in range(CHUNK):
            mixed = mix_s[(c + 1) * CHUNK + t]
            power = jnp.where(
                place == t, jnp.sum(mixed * mixed, axis=1, keepdims=True), power
            )
        return power

    def mix_chunk(c, far):
        for t in range(CHUNK):
            at = c * CHUNK + t
            y = y_ref[at] + over_modes(out_pow[t] * far)
            mix_s[at + CHUNK] = qs_ref[at] * y
        return decay_chunk * far

    def mix_pair(p, carry, base):
        far, power = carry
        power = with_power_of(2 * p - 1, power, base)
        far = mix_chunk(2 * p, far) + first * (p == 0).astype(F32)
        power = with_power_of(2 * p, power, base)
        return mix_chunk(2 * p + 1, far), power

    no_power = jnp.zeros((SEG, LANES), F32)
    mix_s[0:CHUNK] = jnp.zeros((CHUNK, SEG, width), F32)
    far = start + lead * per_mode(incoming)
    far, power_0 = lax.fori_loop(
        0, half // 2, functools.partial(mix_pair, base=0), (far, no_power)
    )
    power_0 = with_power_of(half - 1, power_0, 0)
    _, power_1 = lax.fori_loop(
        half // 2, half, functools.partial(mix_pair, base=half), (far, no_power)
    )
    power_1 = with_power_of(chunks - 1, power_1, half)

    own = jnp.concatenate([power_0, power_1], axis=0)
    send_x[...] = own.astype(BF16)
    over_x = [
        pltpu.make_async_remote_copy(
            src_ref=send_x,
            dst_ref=got_x.at[k],
            send_sem=x_s,
            recv_sem=x_r,
            device_id=along_x(k),
            device_id_type=MESH,
        )
        for k in range(1, X_CHIPS)
    ]
    for copy in over_x:
        copy.start()

    def relayout(c, carry):
        at = pl.ds(pl.multiple_of((c + 1) * CHUNK, CHUNK), CHUNK)
        by_segment = jnp.swapaxes(mix_s[at] * gain, 0, 1)
        for s in range(SEG):
            to = pl.multiple_of(s * steps + c * CHUNK, CHUNK)
            mix_ref[pl.ds(to, CHUNK), :] = by_segment[s]
        return carry

    lax.fori_loop(0, chunks, relayout, 0)
    for k in range(1, n_ctx):
        pl.when(ctx < n_ctx - k)(states[k - 1].wait_send)
    all_of(got_x, x_r)
    own = own + sum(got_x[k].astype(F32) for k in range(1, X_CHIPS))
    send_z[...] = own.astype(BF16)
    over_z = [
        pltpu.make_async_remote_copy(
            src_ref=send_z,
            dst_ref=got_z.at[k],
            send_sem=z_s,
            recv_sem=z_r,
            device_id=along_z(k),
            device_id_type=MESH,
        )
        for k in range(1, z_chips)
    ]
    pl.semaphore_wait(near_sem.at[5], 2)
    for copy in over_z:
        copy.start()
    all_of(got_x, x_s)
    all_of(got_z, z_s)
    all_of(got_z, z_r)
    terms = [own] + [got_z[k].astype(F32) for k in range(1, z_chips)]
    while len(terms) > 1:
        terms = [sum(terms[i : i + 2]) for i in range(0, len(terms), 2)]
    sum_ref[...] = terms[0]


def finish(channels, mix_ref, sum_ref, out_hbm, out_v, out_sem):
    groups = sum_ref.shape[0]
    scale = lax.rsqrt(sum_ref[...] * (1.0 / channels) + 1e-05)
    halves = groups // SEG
    outs = []
    for g in range(groups):
        row = (g % halves) * SEG + g // halves
        spread = jnp.broadcast_to(scale[row : row + 1], (LANES, LANES)).T
        at = pl.ds(g * LANES, LANES)
        out_v[at, :] = (mix_ref[at, :] * spread).astype(BF16)
        if g % 4 == 3:
            span = pl.ds((g - 3) * LANES, 4 * LANES)
            copy = pltpu.make_async_copy(out_v.at[span], out_hbm.at[span], out_sem.at[g // 4])
            copy.start()
            outs.append(copy)
    for copy in outs:
        copy.wait()


def shards(n_ctx, n_chan, queries, keys_in, values_in, short_weights, decay_rates, residues, skip_term, out_gain):
    rows, width = queries.shape[1:]
    taps, modes = short_weights.shape[1], decay_rates.shape[0]
    steps, groups = rows // SEG, rows // LANES
    z_chips = n_chan // X_CHIPS
    dma = pltpu.SemaphoreType.DMA
    vmem = pl.BlockSpec(memory_space=pltpu.VMEM)
    hbm = pl.BlockSpec(memory_space=pltpu.HBM)
    mixed, sums = pl.pallas_call(
        functools.partial(body, (n_ctx, n_chan, width, taps, modes)),
        out_shape=(
            jax.ShapeDtypeStruct((rows, width), F32),
            jax.ShapeDtypeStruct((groups, LANES), F32),
        ),
        in_specs=[hbm] * 8,
        out_specs=(vmem, vmem),
        scratch_shapes=[
            pltpu.VMEM((3, SEG, steps, width), BF16),
            pltpu.VMEM((3, taps, width), F32),
            pltpu.VMEM((modes, width), F32),
            pltpu.VMEM((modes, width), F32),
            pltpu.VMEM((1, width), F32),
            pltpu.VMEM((1, width), F32),
            pltpu.VMEM((3, HALO, width), BF16),
            pltpu.VMEM((steps, SEG, width), F32),
            pltpu.VMEM((steps, SEG, width), F32),
            pltpu.VMEM((steps, SEG, width), F32),
            pltpu.VMEM((steps + CHUNK, SEG, width), F32),
            pltpu.VMEM((steps // KEPT, modes, SEG, width), F32),
            pltpu.VMEM((CHUNK, modes, SEG, width), F32),
            pltpu.VMEM((4, modes, SEG, width), F32),
            pltpu.VMEM((modes, width), BF16),
            pltpu.VMEM((n_ctx, modes, width), BF16),
            pltpu.VMEM((groups, LANES), BF16),
            pltpu.VMEM((X_CHIPS, groups, LANES), BF16),
            pltpu.VMEM((groups, LANES), BF16),
            pltpu.VMEM((z_chips, groups, LANES), BF16),
            dma((3, 2)),
            dma((5,)),
            dma((3,)),
            dma((3,)),
            dma((n_ctx,)),
            dma((n_ctx,)),
            dma,
            dma,
            dma,
            dma,
            pltpu.SemaphoreType.REGULAR((6,)),
        ],
        compiler_params=pltpu.CompilerParams(
            collective_id=0, has_side_effects=True, vmem_limit_bytes=24 << 20
        ),
        name="hyena",
    )(
        *(
            pltpu.with_memory_space_constraint(x, pltpu.HBM)
            for x in (
                queries.reshape(SEG, steps, width),
                keys_in.reshape(SEG, steps, width),
                values_in.reshape(SEG, steps, width),
                short_weights,
                decay_rates,
                residues,
                skip_term[None],
                out_gain[None],
            )
        )
    )
    out = pl.pallas_call(
        functools.partial(finish, width * n_chan),
        out_shape=jax.ShapeDtypeStruct((rows, width), BF16),
        in_specs=[vmem, vmem],
        out_specs=hbm,
        scratch_shapes=[pltpu.VMEM((rows, width), BF16), dma((groups // 4,))],
        compiler_params=pltpu.CompilerParams(vmem_limit_bytes=8 << 20),
        name="finish",
    )(mixed, sums)
    return out[None]


def solution(mesh):
    placed = (
        P(None, "ctx", "chan"),
        P(None, "ctx", "chan"),
        P(None, "ctx", "chan"),
        P(None, None, "chan"),
        P(None, "chan"),
        P(None, "chan"),
        P("chan"),
        P("chan"),
    )
    return jax.shard_map(
        functools.partial(shards, mesh.shape["ctx"], mesh.shape["chan"]),
        mesh=mesh,
        in_specs=placed,
        out_specs=P(None, "ctx", "chan"),
        check_vma=False,
    )
```

```python
import functools

import jax
import jax.numpy as jnp
from jax import lax
from jax.experimental import pallas as pl
from jax.experimental.pallas import tpu as pltpu
from jax.sharding import PartitionSpec as P

MESH = pl.DeviceIdType.MESH
F32 = jnp.float32
BF16 = jnp.bfloat16
SEG = 8
LANES = 128
CHUNK = 16
KEPT = 4
HALO = 16
X_CHIPS = 4


def expm1_of_minus(x):
    series = jnp.full_like(x, 1.0 / 40320.0)
    for factor in (5040.0, 720.0, 120.0, 24.0, 6.0, 2.0, 1.0):
        series = 1.0 / factor - x * series
    return jnp.where(x < 0.25, x * series, 1.0 - jnp.exp(-x))


def per_mode(rows):
    return jnp.broadcast_to(rows[:, None, :], (rows.shape[0], SEG, rows.shape[1]))


def over_modes(terms):
    while terms.shape[0] > 1:
        half = terms.shape[0] // 2
        terms = terms[:half] + terms[half:]
    return terms[0]


def in_all(row):
    return jnp.broadcast_to(row, (SEG, row.shape[-1]))


def body(
    sizes,
    q_hbm,
    k_hbm,
    v_hbm,
    w_hbm,
    lam_hbm,
    res_hbm,
    skip_hbm,
    gain_hbm,
    mix_ref,
    sum_ref,
    raw,
    w_ref,
    lam_ref,
    res_ref,
    skip_ref,
    gain_ref,
    halo,
    u_ref,
    qs_ref,
    y_ref,
    mix_s,
    kept,
    out_pow,
    scan_w,
    send_state,
    got_state,
    send_x,
    got_x,
    send_z,
    got_z,
    in_sem,
    par_sem,
    halo_s,
    halo_r,
    st_s,
    st_r,
    x_s,
    x_r,
    z_s,
    z_r,
    near_sem,
):
    n_ctx, n_chan, width, taps, modes = sizes
    steps = q_hbm.shape[1]
    rows = SEG * steps
    chunks = steps // CHUNK
    rim = taps - 1
    z_chips = n_chan // X_CHIPS
    ctx = lax.axis_index("ctx")
    chan = lax.axis_index("chan")
    my_x, my_z = lax.div(chan, z_chips), lax.rem(chan, z_chips)
    y_chips = n_ctx // 2
    my_y, my_core = lax.div(ctx, 2), lax.rem(ctx, 2)

    def along_ctx(k):
        return (lax.rem(ctx + k, n_ctx), chan)

    def along_y(k, core):
        return (2 * lax.rem(my_y + (k + y_chips), y_chips) + core, chan)

    def along_x(k):
        return (ctx, lax.rem(my_x + (k + X_CHIPS), X_CHIPS) * z_chips + my_z)

    def along_z(k):
        return (ctx, my_x * z_chips + lax.rem(my_z + (k + z_chips), z_chips))

    def all_of(got, *sems):
        part = got.at[pl.ds(1, got.shape[0] - 1)]
        for sem in sems:
            pltpu.make_async_copy(part, part, sem).wait()

    def tell(sem, *others):
        for other in others:
            pl.semaphore_signal(sem, inc=1, device_id=other, device_id_type=MESH)

    streams = (q_hbm, k_hbm, v_hbm)
    params = [
        pltpu.make_async_copy(src, dst, par_sem.at[i])
        for i, (src, dst) in enumerate(
            (
                (w_hbm, w_ref),
                (lam_hbm, lam_ref),
                (res_hbm, res_ref),
                (skip_hbm, skip_ref),
                (gain_hbm, gain_ref),
            )
        )
    ]
    loads = [
        [
            pltpu.make_async_copy(
                streams[i].at[:, pl.ds(h * (steps // 2), steps // 2)],
                raw.at[i, :, pl.ds(h * (steps // 2), steps // 2)],
                in_sem.at[i, h],
            )
            for h in range(2)
        ]
        for i in range(3)
    ]
    for copy in params:
        copy.start()
    for h in range(2):
        loads[1][h].start()
        loads[2][h].start()
    for h in range(2):
        loads[0][h].start()

    barrier = pltpu.get_barrier_semaphore()
    second = my_core == 1
    pl.when(second)(lambda: tell(barrier, along_y(1, 1)))
    tell(
        barrier,
        along_y(0, 1 - my_core),
        along_y(-1, 1),
        along_x(-1),
        along_x(1),
        along_z(-1),
        along_z(1),
    )
    for copy in params:
        copy.wait()

    lam = lam_ref[...]
    coef = res_ref[...] * jnp.sqrt(expm1_of_minus(2.0 * lam))
    decay = 1.0 - expm1_of_minus(lam)
    decay_b = per_mode(decay)

    segment = lax.broadcasted_iota(jnp.int32, (modes, SEG, width), 1)
    for i in range(3):
        weight = per_mode(jnp.exp(lam * (-1.0 * steps * 2**i)))
        scan_w[i] = jnp.where(segment >= 2**i, weight, 0.0)
    scan_w[3] = per_mode(jnp.exp(lam * (-1.0 * (steps - CHUNK))))

    def by_step(i, c):
        part = raw[i, :, pl.ds(pl.multiple_of(c * CHUNK, CHUNK), CHUNK), :]
        return jnp.swapaxes(part.astype(F32), 0, 1)

    def taps_of(i):
        return [in_all(w_ref[i, j : j + 1, :]) for j in range(taps)]

    def filtered(weights, window):
        total = weights[0][None] * window[rim:]
        for j in range(1, taps):
            total = total + weights[j][None] * window[rim - j : rim - j + CHUNK]
        return total

    def make_u(c, before_k, before_v):
        window_k = jnp.concatenate([before_k, by_step(1, c)], axis=0)
        window_v = jnp.concatenate([before_v, by_step(2, c)], axis=0)
        at = pl.ds(pl.multiple_of(c * CHUNK, CHUNK), CHUNK)
        u_ref[at] = filtered(w_k, window_k) * filtered(w_v, window_v)
        return window_k[CHUNK:], window_v[CHUNK:]

    def u_chunk(c, before):
        return make_u(c, *before)

    for i in (1, 2):
        loads[i][0].wait()
    w_k, w_v = taps_of(1), taps_of(2)
    first_k, first_v = by_step(1, 0)[CHUNK - rim :], by_step(2, 0)[CHUNK - rim :]

    halos = [
        pltpu.make_async_remote_copy(
            src_ref=streams[i].at[SEG - 1, pl.ds(steps - HALO, HALO)],
            dst_ref=halo.at[i],
            send_sem=halo_s.at[i],
            recv_sem=halo_r.at[i],
            device_id=along_ctx(1),
            device_id_type=MESH,
        )
        for i in range(3)
    ]

    def pass_on():
        for copy in halos:
            copy.start()
        tell(near_sem.at[1], along_x(-1), along_x(1))
        tell(near_sem.at[2], along_z(-1), along_z(1))

    @pl.when(second)
    def _():
        pl.semaphore_wait(barrier, 8)
        tell(near_sem.at[0], along_y(-1, 1), along_y(1, 1))
        pass_on()

    before = lax.fori_loop(1, chunks // 2, u_chunk, (first_k, first_v))

    for i in (1, 2):
        loads[i][1].wait()
    tail_k, tail_v = lax.fori_loop(chunks // 2, chunks, u_chunk, before)

    @pl.when(second)
    def _():
        pl.semaphore_wait(near_sem.at[0], 2)
        tell(near_sem.at[3], along_y(-2, 1), along_y(2, 1))

    @pl.when(jnp.logical_not(second))
    def _():
        pl.semaphore_wait(barrier, 5)
        pass_on()


    def advance(c, state):
        for t in range(CHUNK):
            at = c * CHUNK + t
            if t % KEPT == 0:
                kept[c * (CHUNK // KEPT) + t // KEPT] = state
            state = decay_b * state + u_ref[at][None]
        return state

    zero_state = jnp.zeros((modes, SEG, width), F32)
    ends = lax.fori_loop(1, chunks, advance, zero_state)

    pl.semaphore_wait(near_sem.at[1], 2)
    pl.semaphore_wait(near_sem.at[2], 2)
    tell(near_sem.at[4], along_z(-2), along_z(2))
    for copy in halos:
        copy.wait()
    has_before = (ctx > 0).astype(F32)
    top = lax.broadcasted_iota(jnp.int32, (rim, SEG, width), 1) == 0

    def entering(i, tail):
        rows_before = halo[i].astype(F32)[HALO - rim :] * has_before
        spread = jnp.broadcast_to(rows_before[:, None, :], (rim, SEG, width))
        return jnp.where(top, spread, pltpu.roll(tail, 1, 1))

    make_u(0, entering(1, tail_k), entering(2, tail_v))
    first = advance(0, zero_state)
    total = ends + scan_w[3] * first
    for i in range(3):
        total = total + scan_w[i] * pltpu.roll(total, 2**i, 1)
    start = jnp.where(segment >= 1, pltpu.roll(total, 1, 1), 0.0)
    end = total[:, SEG - 1, :]
    device_decay = jnp.exp(lam * (-1.0 * rows))

    inward = pltpu.make_async_remote_copy(
        src_ref=send_state,
        dst_ref=got_state.at[0],
        send_sem=st_s.at[0],
        recv_sem=st_r.at[0],
        device_id=along_ctx(1),
        device_id_type=MESH,
    )
    outward = {
        (k, core): pltpu.make_async_remote_copy(
            src_ref=send_state,
            dst_ref=got_state.at[k],
            send_sem=st_s.at[2 * k + core],
            recv_sem=st_r.at[k],
            device_id=along_y(k, core),
            device_id_type=MESH,
        )
        for k in range(1, y_chips)
        for core in range(2)
    }
    sends = {key: jnp.logical_and(second, my_y < y_chips - key[0]) for key in outward}

    @pl.when(jnp.logical_not(second))
    def _():
        send_state[...] = end.astype(BF16)
        inward.start()

    @pl.when(second)
    def _():
        inward.wait_recv()
        send_state[...] = (device_decay * got_state[0].astype(F32) + end).astype(BF16)
        pl.semaphore_wait(near_sem.at[3], 2)

    for key in sorted(outward, key=lambda key: abs(key[0] - y_chips // 2)):
        pl.when(sends[key])(outward[key].start)

    for copy in loads[0]:
        copy.wait()
    w_q = taps_of(0)

    def q_chunk(c, before_q):
        window = jnp.concatenate([before_q, by_step(0, c)], axis=0)
        at = pl.ds(pl.multiple_of(c * CHUNK, CHUNK), CHUNK)
        qs_ref[at] = filtered(w_q, window)
        return window[CHUNK:]

    tail_q = by_step(0, chunks - 1)[CHUNK - rim :]
    lax.fori_loop(0, chunks, q_chunk, entering(0, tail_q))

    pl.semaphore_wait(near_sem.at[4], 2)
    tell(near_sem.at[5], along_z(-4), along_z(4))

    response = []
    power_of = coef
    for i in range(CHUNK):
        if i < KEPT:
            response.append(in_all(jnp.sum(power_of, axis=0, keepdims=True)))
        power_of = power_of * decay
        out_pow[i] = per_mode(power_of)
    response[0] = response[0] + in_all(skip_ref[...])

    def y_chunk(c, carry):
        for b in range(CHUNK // KEPT):
            state = kept[c * (CHUNK // KEPT) + b]
            for i in range(KEPT):
                at = c * CHUNK + b * KEPT + i
                y = over_modes(out_pow[i] * state)
                for j in range(i + 1):
                    y = y + response[j] * u_ref[at - j]
                y_ref[at] = y
        return carry

    lax.fori_loop(0, chunks, y_chunk, 0)

    lead = jnp.exp(per_mode(lam) * (-1.0 * steps * segment.astype(F32)))
    decay_chunk = per_mode(jnp.exp(lam * (-1.0 * CHUNK)))
    reach = [
        jnp.where(my_y >= k, jnp.exp(lam * (-2.0 * rows * (k - 1))), 0.0)
        for k in range(1, y_chips)
    ]
    for k in range(1, y_chips):
        pl.when(my_y >= k)(outward[k, 0].wait_recv)
    terms = [
        jnp.where(my_y >= k, got_state[k].astype(F32), 0.0) * reach[k - 1]
        for k in range(1, y_chips)
    ]
    while len(terms) > 1:
        terms = [sum(terms[i : i + 2]) for i in range(0, len(terms), 2)]
    of_core_0 = jnp.where(second, got_state[0].astype(F32), 0.0)
    incoming = jnp.where(second, device_decay, 1.0) * terms[0] + of_core_0

    lane = lax.broadcasted_iota(jnp.int32, (SEG, LANES), 1)
    gain = in_all(gain_ref[...])

    half = chunks // 2

    def with_power_of(c, power, base):
        place = lane - (c - base) * CHUNK
        for t in range(CHUNK):
            mixed = mix_s[(c + 1) * CHUNK + t]
            power = jnp.where(
                place == t, jnp.sum(mixed * mixed, axis=1, keepdims=True), power
            )
        return power

    def mix_chunk(c, far):
        for t in range(CHUNK):
            at = c * CHUNK + t
            y = y_ref[at] + over_modes(out_pow[t] * far)
            mix_s[at + CHUNK] = qs_ref[at] * y
        return decay_chunk * far

    def mix_pair(p, carry, base):
        far, power = carry
        power = with_power_of(2 * p - 1, power, base)
        far = mix_chunk(2 * p, far) + first * (p == 0).astype(F32)
        power = with_power_of(2 * p, power, base)
        return mix_chunk(2 * p + 1, far), power

    no_power = jnp.zeros((SEG, LANES), F32)
    mix_s[0:CHUNK] = jnp.zeros((CHUNK, SEG, width), F32)
    far = start + lead * per_mode(incoming)
    far, power_0 = lax.fori_loop(
        0, half // 2, functools.partial(mix_pair, base=0), (far, no_power)
    )
    power_0 = with_power_of(half - 1, power_0, 0)
    _, power_1 = lax.fori_loop(
        half // 2, half, functools.partial(mix_pair, base=half), (far, no_power)
    )
    power_1 = with_power_of(chunks - 1, power_1, half)

    own = jnp.concatenate([power_0, power_1], axis=0)
    send_x[...] = own.astype(BF16)
    over_x = [
        pltpu.make_async_remote_copy(
            src_ref=send_x,
            dst_ref=got_x.at[k],
            send_sem=x_s,
            recv_sem=x_r,
            device_id=along_x(k),
            device_id_type=MESH,
        )
        for k in range(1, X_CHIPS)
    ]
    for copy in over_x:
        copy.start()

    def relayout(c, carry):
        at = pl.ds(pl.multiple_of((c + 1) * CHUNK, CHUNK), CHUNK)
        by_segment = jnp.swapaxes(mix_s[at] * gain, 0, 1)
        for s in range(SEG):
            to = pl.multiple_of(s * steps + c * CHUNK, CHUNK)
            mix_ref[pl.ds(to, CHUNK), :] = by_segment[s]
        return carry

    lax.fori_loop(0, chunks, relayout, 0)
    pl.when(jnp.logical_not(second))(inward.wait_send)
    for key in outward:
        pl.when(sends[key])(outward[key].wait_send)
    all_of(got_x, x_r)
    own = own + sum(got_x[k].astype(F32) for k in range(1, X_CHIPS))
    send_z[...] = own.astype(BF16)
    over_z = [
        pltpu.make_async_remote_copy(
            src_ref=send_z,
            dst_ref=got_z.at[k],
            send_sem=z_s,
            recv_sem=z_r,
            device_id=along_z(k),
            device_id_type=MESH,
        )
        for k in range(1, z_chips)
    ]
    pl.semaphore_wait(near_sem.at[5], 2)
    for copy in over_z:
        copy.start()
    all_of(got_x, x_s)
    all_of(got_z, z_s)
    all_of(got_z, z_r)
    terms = [own] + [got_z[k].astype(F32) for k in range(1, z_chips)]
    while len(terms) > 1:
        terms = [sum(terms[i : i + 2]) for i in range(0, len(terms), 2)]
    sum_ref[...] = terms[0]


def finish(channels, mix_ref, sum_ref, out_hbm, out_v, out_sem):
    groups = sum_ref.shape[0]
    scale = lax.rsqrt(sum_ref[...] * (1.0 / channels) + 1e-05)
    halves = groups // SEG
    outs = []
    for g in range(groups):
        row = (g % halves) * SEG + g // halves
        spread = jnp.broadcast_to(scale[row : row + 1], (LANES, LANES)).T
        at = pl.ds(g * LANES, LANES)
        out_v[at, :] = (mix_ref[at, :] * spread).astype(BF16)
        if g % 4 == 3:
            span = pl.ds((g - 3) * LANES, 4 * LANES)
            copy = pltpu.make_async_copy(out_v.at[span], out_hbm.at[span], out_sem.at[g // 4])
            copy.start()
            outs.append(copy)
    for copy in outs:
        copy.wait()


def shards(n_ctx, n_chan, queries, keys_in, values_in, short_weights, decay_rates, residues, skip_term, out_gain):
    rows, width = queries.shape[1:]
    taps, modes = short_weights.shape[1], decay_rates.shape[0]
    steps, groups = rows // SEG, rows // LANES
    z_chips = n_chan // X_CHIPS
    dma = pltpu.SemaphoreType.DMA
    vmem = pl.BlockSpec(memory_space=pltpu.VMEM)
    hbm = pl.BlockSpec(memory_space=pltpu.HBM)
    mixed, sums = pl.pallas_call(
        functools.partial(body, (n_ctx, n_chan, width, taps, modes)),
        out_shape=(
            jax.ShapeDtypeStruct((rows, width), F32),
            jax.ShapeDtypeStruct((groups, LANES), F32),
        ),
        in_specs=[hbm] * 8,
        out_specs=(vmem, vmem),
        scratch_shapes=[
            pltpu.VMEM((3, SEG, steps, width), BF16),
            pltpu.VMEM((3, taps, width), F32),
            pltpu.VMEM((modes, width), F32),
            pltpu.VMEM((modes, width), F32),
            pltpu.VMEM((1, width), F32),
            pltpu.VMEM((1, width), F32),
            pltpu.VMEM((3, HALO, width), BF16),
            pltpu.VMEM((steps, SEG, width), F32),
            pltpu.VMEM((steps, SEG, width), F32),
            pltpu.VMEM((steps, SEG, width), F32),
            pltpu.VMEM((steps + CHUNK, SEG, width), F32),
            pltpu.VMEM((steps // KEPT, modes, SEG, width), F32),
            pltpu.VMEM((CHUNK, modes, SEG, width), F32),
            pltpu.VMEM((4, modes, SEG, width), F32),
            pltpu.VMEM((modes, width), BF16),
            pltpu.VMEM((n_ctx // 2, modes, width), BF16),
            pltpu.VMEM((groups, LANES), BF16),
            pltpu.VMEM((X_CHIPS, groups, LANES), BF16),
            pltpu.VMEM((groups, LANES), BF16),
            pltpu.VMEM((z_chips, groups, LANES), BF16),
            dma((3, 2)),
            dma((5,)),
            dma((3,)),
            dma((3,)),
            dma((n_ctx,)),
            dma((n_ctx // 2,)),
            dma,
            dma,
            dma,
            dma,
            pltpu.SemaphoreType.REGULAR((6,)),
        ],
        compiler_params=pltpu.CompilerParams(
            collective_id=0, has_side_effects=True, vmem_limit_bytes=24 << 20
        ),
        name="hyena",
    )(
        *(
            pltpu.with_memory_space_constraint(x, pltpu.HBM)
            for x in (
                queries.reshape(SEG, steps, width),
                keys_in.reshape(SEG, steps, width),
                values_in.reshape(SEG, steps, width),
                short_weights,
                decay_rates,
                residues,
                skip_term[None],
                out_gain[None],
            )
        )
    )
    out = pl.pallas_call(
        functools.partial(finish, width * n_chan),
        out_shape=jax.ShapeDtypeStruct((rows, width), BF16),
        in_specs=[vmem, vmem],
        out_specs=hbm,
        scratch_shapes=[pltpu.VMEM((rows, width), BF16), dma((groups // 4,))],
        compiler_params=pltpu.CompilerParams(vmem_limit_bytes=8 << 20),
        name="finish",
    )(mixed, sums)
    return out[None]


def solution(mesh):
    placed = (
        P(None, "ctx", "chan"),
        P(None, "ctx", "chan"),
        P(None, "ctx", "chan"),
        P(None, None, "chan"),
        P(None, "chan"),
        P(None, "chan"),
        P("chan"),
        P("chan"),
    )
    return jax.shard_map(
        functools.partial(shards, mesh.shape["ctx"], mesh.shape["chan"]),
        mesh=mesh,
        in_specs=placed,
        out_specs=P(None, "ctx", "chan"),
        check_vma=False,
    )
```

```python
import functools

import jax
import jax.numpy as jnp
from jax import lax
from jax.experimental import pallas as pl
from jax.experimental.pallas import tpu as pltpu
from jax.sharding import PartitionSpec as P

MESH = pl.DeviceIdType.MESH
F32 = jnp.float32
BF16 = jnp.bfloat16
SEG = 8
LANES = 128
CHUNK = 16
KEPT = 4
GROUP = 8
BY = (7, 8, 5, 4, 4, 4)
HALO = 16
X_CHIPS = 4


def expm1_of_minus(x):
    series = jnp.full_like(x, 1.0 / 40320.0)
    for factor in (5040.0, 720.0, 120.0, 24.0, 6.0, 2.0, 1.0):
        series = 1.0 / factor - x * series
    return jnp.where(x < 0.25, x * series, 1.0 - jnp.exp(-x))


def per_mode(rows):
    return jnp.broadcast_to(rows[:, None, :], (rows.shape[0], SEG, rows.shape[1]))


def loop(first, last, by, step, carry):
    def some(g, carry):
        for j in range(by):
            carry = step(first + g * by + j, carry)
        return carry

    return lax.fori_loop(0, (last - first) // by, some, carry)


def over_modes(terms):
    while terms.shape[0] > 1:
        half = terms.shape[0] // 2
        terms = terms[:half] + terms[half:]
    return terms[0]


def in_all(row):
    return jnp.broadcast_to(row, (SEG, row.shape[-1]))


def body(
    sizes,
    q_hbm,
    k_hbm,
    v_hbm,
    w_hbm,
    lam_hbm,
    res_hbm,
    skip_hbm,
    gain_hbm,
    mix_ref,
    sum_ref,
    raw,
    w_ref,
    lam_ref,
    res_ref,
    skip_ref,
    gain_ref,
    halo,
    u_ref,
    qs_ref,
    y_ref,
    mix_s,
    kept,
    out_pow,
    scan_w,
    send_state,
    got_state,
    send_x,
    got_x,
    send_z,
    got_z,
    in_sem,
    par_sem,
    halo_s,
    halo_r,
    st_s,
    st_r,
    x_s,
    x_r,
    z_s,
    z_r,
    near_sem,
):
    n_ctx, n_chan, width, taps, modes = sizes
    steps = q_hbm.shape[1]
    rows = SEG * steps
    chunks = steps // CHUNK
    rim = taps - 1
    z_chips = n_chan // X_CHIPS
    ctx = lax.axis_index("ctx")
    chan = lax.axis_index("chan")
    my_x, my_z = lax.div(chan, z_chips), lax.rem(chan, z_chips)
    y_chips = n_ctx // 2
    my_y, my_core = lax.div(ctx, 2), lax.rem(ctx, 2)

    def along_ctx(k):
        return (lax.rem(ctx + k, n_ctx), chan)

    def along_y(k, core):
        return (2 * lax.rem(my_y + (k + y_chips), y_chips) + core, chan)

    def along_x(k):
        return (ctx, lax.rem(my_x + (k + X_CHIPS), X_CHIPS) * z_chips + my_z)

    def along_z(k):
        return (ctx, my_x * z_chips + lax.rem(my_z + (k + z_chips), z_chips))

    def all_of(got, *sems):
        part = got.at[pl.ds(1, got.shape[0] - 1)]
        for sem in sems:
            pltpu.make_async_copy(part, part, sem).wait()

    def tell(sem, *others):
        for other in others:
            pl.semaphore_signal(sem, inc=1, device_id=other, device_id_type=MESH)

    streams = (q_hbm, k_hbm, v_hbm)
    params = [
        pltpu.make_async_copy(src, dst, par_sem.at[i])
        for i, (src, dst) in enumerate(
            (
                (w_hbm, w_ref),
                (lam_hbm, lam_ref),
                (res_hbm, res_ref),
                (skip_hbm, skip_ref),
                (gain_hbm, gain_ref),
            )
        )
    ]
    loads = [
        [
            pltpu.make_async_copy(
                streams[i].at[:, pl.ds(h * (steps // 2), steps // 2)],
                raw.at[i, :, pl.ds(h * (steps // 2), steps // 2)],
                in_sem.at[i, h],
            )
            for h in range(2)
        ]
        for i in range(3)
    ]
    for copy in params:
        copy.start()
    for h in range(2):
        loads[1][h].start()
        loads[2][h].start()
    for h in range(2):
        loads[0][h].start()

    barrier = pltpu.get_barrier_semaphore()
    second = my_core == 1
    pl.when(second)(lambda: tell(barrier, along_y(1, 1)))
    tell(
        barrier,
        along_y(0, 1 - my_core),
        along_y(-1, 1),
        along_x(-1),
        along_x(1),
        along_z(-1),
        along_z(1),
    )
    for copy in params:
        copy.wait()

    lam = lam_ref[...]
    coef = res_ref[...] * jnp.sqrt(expm1_of_minus(2.0 * lam))
    decay = 1.0 - expm1_of_minus(lam)
    decay_b = per_mode(decay)

    segment = lax.broadcasted_iota(jnp.int32, (modes, SEG, width), 1)
    for i in range(3):
        weight = per_mode(jnp.exp(lam * (-1.0 * steps * 2**i)))
        scan_w[i] = jnp.where(segment >= 2**i, weight, 0.0)
    scan_w[3] = per_mode(jnp.exp(lam * (-1.0 * (steps - CHUNK))))

    def by_step(i, c):
        part = raw[i, :, pl.ds(pl.multiple_of(c * CHUNK, CHUNK), CHUNK), :]
        return jnp.swapaxes(part.astype(F32), 0, 1)

    def taps_of(i):
        return [in_all(w_ref[i, j : j + 1, :]) for j in range(taps)]

    def filtered(weights, window):
        total = weights[0][None] * window[rim:]
        for j in range(1, taps):
            total = total + weights[j][None] * window[rim - j : rim - j + CHUNK]
        return total

    def make_u(c, before_k, before_v):
        window_k = jnp.concatenate([before_k, by_step(1, c)], axis=0)
        window_v = jnp.concatenate([before_v, by_step(2, c)], axis=0)
        at = pl.ds(pl.multiple_of(c * CHUNK, CHUNK), CHUNK)
        u_ref[at] = filtered(w_k, window_k) * filtered(w_v, window_v)
        return window_k[CHUNK:], window_v[CHUNK:]

    def u_chunk(c, before):
        return make_u(c, *before)

    for i in (1, 2):
        loads[i][0].wait()
    w_k, w_v = taps_of(1), taps_of(2)
    first_k, first_v = by_step(1, 0)[CHUNK - rim :], by_step(2, 0)[CHUNK - rim :]

    halos = [
        pltpu.make_async_remote_copy(
            src_ref=streams[i].at[SEG - 1, pl.ds(steps - HALO, HALO)],
            dst_ref=halo.at[i],
            send_sem=halo_s.at[i],
            recv_sem=halo_r.at[i],
            device_id=along_ctx(1),
            device_id_type=MESH,
        )
        for i in range(3)
    ]

    def pass_on():
        for copy in halos:
            copy.start()
        tell(near_sem.at[1], along_x(-1), along_x(1))
        tell(near_sem.at[2], along_z(-1), along_z(1))

    @pl.when(second)
    def _():
        pl.semaphore_wait(barrier, 8)
        tell(near_sem.at[0], along_y(-1, 1), along_y(1, 1))
        pass_on()

    before = loop(1, chunks // 2, BY[0], u_chunk, (first_k, first_v))

    for i in (1, 2):
        loads[i][1].wait()
    tail_k, tail_v = loop(chunks // 2, chunks, BY[1], u_chunk, before)

    @pl.when(second)
    def _():
        pl.semaphore_wait(near_sem.at[0], 2)
        tell(near_sem.at[3], along_y(-2, 1), along_y(2, 1))

    @pl.when(jnp.logical_not(second))
    def _():
        pl.semaphore_wait(barrier, 5)
        pass_on()


    def advance(c, state):
        for t in range(CHUNK):
            at = c * CHUNK + t
            if t % KEPT == 0:
                kept[c * (CHUNK // KEPT) + t // KEPT] = state
            state = decay_b * state + u_ref[at][None]
        return state

    zero_state = jnp.zeros((modes, SEG, width), F32)
    ends = loop(1, chunks, BY[2], advance, zero_state)

    pl.semaphore_wait(near_sem.at[1], 2)
    pl.semaphore_wait(near_sem.at[2], 2)
    tell(near_sem.at[4], along_z(-2), along_z(2))
    for copy in halos:
        copy.wait()
    has_before = (ctx > 0).astype(F32)
    top = lax.broadcasted_iota(jnp.int32, (rim, SEG, width), 1) == 0

    def entering(i, tail):
        rows_before = halo[i].astype(F32)[HALO - rim :] * has_before
        spread = jnp.broadcast_to(rows_before[:, None, :], (rim, SEG, width))
        return jnp.where(top, spread, pltpu.roll(tail, 1, 1))

    make_u(0, entering(1, tail_k), entering(2, tail_v))
    first = advance(0, zero_state)
    total = ends + scan_w[3] * first
    for i in range(3):
        total = total + scan_w[i] * pltpu.roll(total, 2**i, 1)
    start = jnp.where(segment >= 1, pltpu.roll(total, 1, 1), 0.0)
    end = total[:, SEG - 1, :]
    device_decay = jnp.exp(lam * (-1.0 * rows))

    inward = pltpu.make_async_remote_copy(
        src_ref=send_state,
        dst_ref=got_state.at[0],
        send_sem=st_s.at[0],
        recv_sem=st_r.at[0],
        device_id=along_ctx(1),
        device_id_type=MESH,
    )
    outward = {
        (k, core): pltpu.make_async_remote_copy(
            src_ref=send_state,
            dst_ref=got_state.at[k],
            send_sem=st_s.at[2 * k + core],
            recv_sem=st_r.at[k],
            device_id=along_y(k, core),
            device_id_type=MESH,
        )
        for k in range(1, y_chips)
        for core in range(2)
    }
    sends = {key: jnp.logical_and(second, my_y < y_chips - key[0]) for key in outward}

    @pl.when(jnp.logical_not(second))
    def _():
        send_state[...] = end.astype(BF16)
        inward.start()

    @pl.when(second)
    def _():
        inward.wait_recv()
        send_state[...] = (device_decay * got_state[0].astype(F32) + end).astype(BF16)
        pl.semaphore_wait(near_sem.at[3], 2)

    for key in sorted(outward, key=lambda key: abs(key[0] - y_chips // 2)):
        pl.when(sends[key])(outward[key].start)

    for copy in loads[0]:
        copy.wait()
    w_q = taps_of(0)

    def q_chunk(c, before_q):
        window = jnp.concatenate([before_q, by_step(0, c)], axis=0)
        at = pl.ds(pl.multiple_of(c * CHUNK, CHUNK), CHUNK)
        qs_ref[at] = filtered(w_q, window)
        return window[CHUNK:]

    tail_q = by_step(0, chunks - 1)[CHUNK - rim :]
    loop(0, chunks, BY[3], q_chunk, entering(0, tail_q))

    pl.semaphore_wait(near_sem.at[4], 2)
    tell(near_sem.at[5], along_z(-4), along_z(4))

    response = []
    power_of = coef
    for i in range(CHUNK):
        if i < KEPT:
            response.append(in_all(jnp.sum(power_of, axis=0, keepdims=True)))
        power_of = power_of * decay
        out_pow[i] = per_mode(power_of)
    response[0] = response[0] + in_all(skip_ref[...])

    def y_chunk(c, carry):
        for b in range(CHUNK // KEPT):
            state = kept[c * (CHUNK // KEPT) + b]
            for i in range(KEPT):
                at = c * CHUNK + b * KEPT + i
                y = over_modes(out_pow[i] * state)
                for j in range(i + 1):
                    y = y + response[j] * u_ref[at - j]
                y_ref[at] = y
        return carry

    loop(0, chunks, BY[4], y_chunk, 0)

    lead = jnp.exp(per_mode(lam) * (-1.0 * steps * segment.astype(F32)))
    decay_chunk = per_mode(jnp.exp(lam * (-1.0 * CHUNK)))
    reach = [
        jnp.where(my_y >= k, jnp.exp(lam * (-2.0 * rows * (k - 1))), 0.0)
        for k in range(1, y_chips)
    ]
    for k in range(1, y_chips):
        pl.when(my_y >= k)(outward[k, 0].wait_recv)
    terms = [
        jnp.where(my_y >= k, got_state[k].astype(F32), 0.0) * reach[k - 1]
        for k in range(1, y_chips)
    ]
    while len(terms) > 1:
        terms = [sum(terms[i : i + 2]) for i in range(0, len(terms), 2)]
    of_core_0 = jnp.where(second, got_state[0].astype(F32), 0.0)
    incoming = jnp.where(second, device_decay, 1.0) * terms[0] + of_core_0

    lane = lax.broadcasted_iota(jnp.int32, (SEG, LANES), 1)
    gain = in_all(gain_ref[...])

    half = chunks // 2

    def with_power_of(c, power, base):
        place = lane - (c - base) * CHUNK
        for t in range(CHUNK):
            mixed = mix_s[(c + 1) * CHUNK + t]
            power = jnp.where(
                place == t, jnp.sum(mixed * mixed, axis=1, keepdims=True), power
            )
        return power

    def mix_chunk(c, far):
        for t in range(CHUNK):
            at = c * CHUNK + t
            y = y_ref[at] + over_modes(out_pow[t] * far)
            mix_s[at + CHUNK] = qs_ref[at] * y
        return decay_chunk * far

    def mix_group(p, carry, base):
        far, power = carry
        for j in range(GROUP):
            power = with_power_of(GROUP * p + j - 1, power, base)
            far = mix_chunk(GROUP * p + j, far)
            if j == 0:
                far = far + first * (p == 0).astype(F32)
        return far, power

    no_power = jnp.zeros((SEG, LANES), F32)
    mix_s[0:CHUNK] = jnp.zeros((CHUNK, SEG, width), F32)
    far = start + lead * per_mode(incoming)
    far, power_0 = lax.fori_loop(
        0, half // GROUP, functools.partial(mix_group, base=0), (far, no_power)
    )
    power_0 = with_power_of(half - 1, power_0, 0)
    _, power_1 = lax.fori_loop(
        half // GROUP, chunks // GROUP, functools.partial(mix_group, base=half), (far, no_power)
    )
    power_1 = with_power_of(chunks - 1, power_1, half)

    own = jnp.concatenate([power_0, power_1], axis=0)
    send_x[...] = own.astype(BF16)
    over_x = [
        pltpu.make_async_remote_copy(
            src_ref=send_x,
            dst_ref=got_x.at[k],
            send_sem=x_s,
            recv_sem=x_r,
            device_id=along_x(k),
            device_id_type=MESH,
        )
        for k in range(1, X_CHIPS)
    ]
    for copy in over_x:
        copy.start()

    def relayout(c, carry):
        at = pl.ds(pl.multiple_of((c + 1) * CHUNK, CHUNK), CHUNK)
        by_segment = jnp.swapaxes(mix_s[at] * gain, 0, 1)
        for s in range(SEG):
            to = pl.multiple_of(s * steps + c * CHUNK, CHUNK)
            mix_ref[pl.ds(to, CHUNK), :] = by_segment[s]
        return carry

    loop(0, chunks, BY[5], relayout, 0)
    pl.when(jnp.logical_not(second))(inward.wait_send)
    for key in outward:
        pl.when(sends[key])(outward[key].wait_send)
    all_of(got_x, x_r)
    own = own + sum(got_x[k].astype(F32) for k in range(1, X_CHIPS))
    send_z[...] = own.astype(BF16)
    over_z = [
        pltpu.make_async_remote_copy(
            src_ref=send_z,
            dst_ref=got_z.at[k],
            send_sem=z_s,
            recv_sem=z_r,
            device_id=along_z(k),
            device_id_type=MESH,
        )
        for k in range(1, z_chips)
    ]
    pl.semaphore_wait(near_sem.at[5], 2)
    for copy in over_z:
        copy.start()
    all_of(got_x, x_s)
    all_of(got_z, z_s)
    all_of(got_z, z_r)
    terms = [own] + [got_z[k].astype(F32) for k in range(1, z_chips)]
    while len(terms) > 1:
        terms = [sum(terms[i : i + 2]) for i in range(0, len(terms), 2)]
    sum_ref[...] = terms[0]


def finish(channels, mix_ref, sum_ref, out_hbm, out_v, out_sem):
    groups = sum_ref.shape[0]
    scale = lax.rsqrt(sum_ref[...] * (1.0 / channels) + 1e-05)
    halves = groups // SEG
    outs = []
    for g in range(groups):
        row = (g % halves) * SEG + g // halves
        spread = jnp.broadcast_to(scale[row : row + 1], (LANES, LANES)).T
        at = pl.ds(g * LANES, LANES)
        out_v[at, :] = (mix_ref[at, :] * spread).astype(BF16)
        if g % 4 == 3:
            span = pl.ds((g - 3) * LANES, 4 * LANES)
            copy = pltpu.make_async_copy(out_v.at[span], out_hbm.at[span], out_sem.at[g // 4])
            copy.start()
            outs.append(copy)
    for copy in outs:
        copy.wait()


def shards(n_ctx, n_chan, queries, keys_in, values_in, short_weights, decay_rates, residues, skip_term, out_gain):
    rows, width = queries.shape[1:]
    taps, modes = short_weights.shape[1], decay_rates.shape[0]
    steps, groups = rows // SEG, rows // LANES
    z_chips = n_chan // X_CHIPS
    dma = pltpu.SemaphoreType.DMA
    vmem = pl.BlockSpec(memory_space=pltpu.VMEM)
    hbm = pl.BlockSpec(memory_space=pltpu.HBM)
    mixed, sums = pl.pallas_call(
        functools.partial(body, (n_ctx, n_chan, width, taps, modes)),
        out_shape=(
            jax.ShapeDtypeStruct((rows, width), F32),
            jax.ShapeDtypeStruct((groups, LANES), F32),
        ),
        in_specs=[hbm] * 8,
        out_specs=(vmem, vmem),
        scratch_shapes=[
            pltpu.VMEM((3, SEG, steps, width), BF16),
            pltpu.VMEM((3, taps, width), F32),
            pltpu.VMEM((modes, width), F32),
            pltpu.VMEM((modes, width), F32),
            pltpu.VMEM((1, width), F32),
            pltpu.VMEM((1, width), F32),
            pltpu.VMEM((3, HALO, width), BF16),
            pltpu.VMEM((steps, SEG, width), F32),
            pltpu.VMEM((steps, SEG, width), F32),
            pltpu.VMEM((steps, SEG, width), F32),
            pltpu.VMEM((steps + CHUNK, SEG, width), F32),
            pltpu.VMEM((steps // KEPT, modes, SEG, width), F32),
            pltpu.VMEM((CHUNK, modes, SEG, width), F32),
            pltpu.VMEM((4, modes, SEG, width), F32),
            pltpu.VMEM((modes, width), BF16),
            pltpu.VMEM((n_ctx // 2, modes, width), BF16),
            pltpu.VMEM((groups, LANES), BF16),
            pltpu.VMEM((X_CHIPS, groups, LANES), BF16),
            pltpu.VMEM((groups, LANES), BF16),
            pltpu.VMEM((z_chips, groups, LANES), BF16),
            dma((3, 2)),
            dma((5,)),
            dma((3,)),
            dma((3,)),
            dma((n_ctx,)),
            dma((n_ctx // 2,)),
            dma,
            dma,
            dma,
            dma,
            pltpu.SemaphoreType.REGULAR((6,)),
        ],
        compiler_params=pltpu.CompilerParams(
            collective_id=0, has_side_effects=True, vmem_limit_bytes=24 << 20
        ),
        name="hyena",
    )(
        *(
            pltpu.with_memory_space_constraint(x, pltpu.HBM)
            for x in (
                queries.reshape(SEG, steps, width),
                keys_in.reshape(SEG, steps, width),
                values_in.reshape(SEG, steps, width),
                short_weights,
                decay_rates,
                residues,
                skip_term[None],
                out_gain[None],
            )
        )
    )
    out = pl.pallas_call(
        functools.partial(finish, width * n_chan),
        out_shape=jax.ShapeDtypeStruct((rows, width), BF16),
        in_specs=[vmem, vmem],
        out_specs=hbm,
        scratch_shapes=[pltpu.VMEM((rows, width), BF16), dma((groups // 4,))],
        compiler_params=pltpu.CompilerParams(vmem_limit_bytes=8 << 20),
        name="finish",
    )(mixed, sums)
    return out[None]


def solution(mesh):
    placed = (
        P(None, "ctx", "chan"),
        P(None, "ctx", "chan"),
        P(None, "ctx", "chan"),
        P(None, None, "chan"),
        P(None, "chan"),
        P(None, "chan"),
        P("chan"),
        P("chan"),
    )
    return jax.shard_map(
        functools.partial(shards, mesh.shape["ctx"], mesh.shape["chan"]),
        mesh=mesh,
        in_specs=placed,
        out_specs=P(None, "ctx", "chan"),
        check_vma=False,
    )
```

```python
import functools

import jax
import jax.numpy as jnp
from jax import lax
from jax.experimental import pallas as pl
from jax.experimental.pallas import tpu as pltpu
from jax.sharding import PartitionSpec as P

MESH = pl.DeviceIdType.MESH
F32 = jnp.float32
BF16 = jnp.bfloat16
SEG = 8
LANES = 128
CHUNK = 16
KEPT = 4
GROUP = 8
BY = (7, 8, 5, 4, 4, 4)
HALO = 16
X_CHIPS = 4


def expm1_of_minus(x):
    series = jnp.full_like(x, 1.0 / 40320.0)
    for factor in (5040.0, 720.0, 120.0, 24.0, 6.0, 2.0, 1.0):
        series = 1.0 / factor - x * series
    return jnp.where(x < 0.25, x * series, 1.0 - jnp.exp(-x))


def per_mode(rows):
    return jnp.broadcast_to(rows[:, None, :], (rows.shape[0], SEG, rows.shape[1]))


def loop(first, last, by, step, carry):
    def some(g, carry):
        for j in range(by):
            carry = step(first + g * by + j, carry)
        return carry

    return lax.fori_loop(0, (last - first) // by, some, carry)


def over_modes(terms):
    while terms.shape[0] > 1:
        half = terms.shape[0] // 2
        terms = terms[:half] + terms[half:]
    return terms[0]


def in_all(row):
    return jnp.broadcast_to(row, (SEG, row.shape[-1]))


def body(
    sizes,
    q_hbm,
    k_hbm,
    v_hbm,
    w_hbm,
    lam_hbm,
    res_hbm,
    skip_hbm,
    gain_hbm,
    mix_ref,
    sum_ref,
    raw,
    w_ref,
    lam_ref,
    res_ref,
    skip_ref,
    gain_ref,
    halo,
    u_ref,
    qs_ref,
    y_ref,
    mix_s,
    kept,
    out_pow,
    scan_w,
    send_state,
    got_state,
    send_x,
    got_x,
    send_z,
    got_z,
    in_sem,
    par_sem,
    halo_s,
    halo_r,
    st_s,
    st_r,
    x_s,
    x_r,
    z_s,
    z_r,
    near_sem,
):
    n_ctx, n_chan, width, taps, modes = sizes
    steps = q_hbm.shape[1]
    rows = SEG * steps
    chunks = steps // CHUNK
    rim = taps - 1
    z_chips = n_chan // X_CHIPS
    ctx = lax.axis_index("ctx")
    chan = lax.axis_index("chan")
    my_x, my_z = lax.div(chan, z_chips), lax.rem(chan, z_chips)
    y_chips = n_ctx // 2
    my_y, my_core = lax.div(ctx, 2), lax.rem(ctx, 2)

    def along_ctx(k):
        return (lax.rem(ctx + k, n_ctx), chan)

    def along_y(k, core):
        return (2 * lax.rem(my_y + (k + y_chips), y_chips) + core, chan)

    def along_x(k):
        return (ctx, lax.rem(my_x + (k + X_CHIPS), X_CHIPS) * z_chips + my_z)

    def along_z(k):
        return (ctx, my_x * z_chips + lax.rem(my_z + (k + z_chips), z_chips))

    def all_of(got, *sems):
        part = got.at[pl.ds(1, got.shape[0] - 1)]
        for sem in sems:
            pltpu.make_async_copy(part, part, sem).wait()

    def tell(sem, *others):
        for other in others:
            pl.semaphore_signal(sem, inc=1, device_id=other, device_id_type=MESH)

    streams = (q_hbm, k_hbm, v_hbm)
    params = [
        pltpu.make_async_copy(src, dst, par_sem.at[i])
        for i, (src, dst) in enumerate(
            (
                (w_hbm, w_ref),
                (lam_hbm, lam_ref),
                (res_hbm, res_ref),
                (skip_hbm, skip_ref),
                (gain_hbm, gain_ref),
            )
        )
    ]
    loads = [
        [
            pltpu.make_async_copy(
                streams[i].at[:, pl.ds(h * (steps // 2), steps // 2)],
                raw.at[i, :, pl.ds(h * (steps // 2), steps // 2)],
                in_sem.at[i, h],
            )
            for h in range(2)
        ]
        for i in range(3)
    ]
    for copy in params:
        copy.start()
    for h in range(2):
        loads[1][h].start()
        loads[2][h].start()
    for h in range(2):
        loads[0][h].start()

    barrier = pltpu.get_barrier_semaphore()
    second = my_core == 1
    pl.when(second)(lambda: tell(barrier, along_y(1, 1)))
    tell(
        barrier,
        along_y(0, 1 - my_core),
        along_y(-1, 1),
        along_x(-1),
        along_x(1),
        along_z(-1),
        along_z(1),
    )
    for copy in params:
        copy.wait()

    lam = lam_ref[...]
    coef = res_ref[...] * jnp.sqrt(expm1_of_minus(2.0 * lam))
    decay = 1.0 - expm1_of_minus(lam)
    decay_b = per_mode(decay)

    segment = lax.broadcasted_iota(jnp.int32, (modes, SEG, width), 1)
    for i in range(3):
        weight = per_mode(jnp.exp(lam * (-1.0 * steps * 2**i)))
        scan_w[i] = jnp.where(segment >= 2**i, weight, 0.0)
    scan_w[3] = per_mode(jnp.exp(lam * (-1.0 * (steps - CHUNK))))

    def by_step(i, c):
        part = raw[i, :, pl.ds(pl.multiple_of(c * CHUNK, CHUNK), CHUNK), :]
        return jnp.swapaxes(part.astype(F32), 0, 1)

    def taps_of(i):
        return [in_all(w_ref[i, j : j + 1, :]) for j in range(taps)]

    def filtered(weights, window):
        total = weights[0][None] * window[rim:]
        for j in range(1, taps):
            total = total + weights[j][None] * window[rim - j : rim - j + CHUNK]
        return total

    def make_u(c, before_k, before_v):
        window_k = jnp.concatenate([before_k, by_step(1, c)], axis=0)
        window_v = jnp.concatenate([before_v, by_step(2, c)], axis=0)
        at = pl.ds(pl.multiple_of(c * CHUNK, CHUNK), CHUNK)
        u_ref[at] = filtered(w_k, window_k) * filtered(w_v, window_v)
        return window_k[CHUNK:], window_v[CHUNK:]

    def u_chunk(c, before):
        return make_u(c, *before)

    for i in (1, 2):
        loads[i][0].wait()
    w_k, w_v = taps_of(1), taps_of(2)
    first_k, first_v = by_step(1, 0)[CHUNK - rim :], by_step(2, 0)[CHUNK - rim :]

    halos = [
        pltpu.make_async_remote_copy(
            src_ref=streams[i].at[SEG - 1, pl.ds(steps - HALO, HALO)],
            dst_ref=halo.at[i],
            send_sem=halo_s.at[i],
            recv_sem=halo_r.at[i],
            device_id=along_ctx(1),
            device_id_type=MESH,
        )
        for i in range(3)
    ]

    def pass_on():
        for copy in halos:
            copy.start()
        tell(near_sem.at[1], along_x(-1), along_x(1))
        tell(near_sem.at[2], along_z(-1), along_z(1))

    @pl.when(second)
    def _():
        pl.semaphore_wait(barrier, 8)
        tell(near_sem.at[0], along_y(-1, 1), along_y(1, 1))
        pass_on()

    before = loop(1, chunks // 2, BY[0], u_chunk, (first_k, first_v))

    for i in (1, 2):
        loads[i][1].wait()
    tail_k, tail_v = loop(chunks // 2, chunks, BY[1], u_chunk, before)

    @pl.when(second)
    def _():
        pl.semaphore_wait(near_sem.at[0], 2)
        tell(near_sem.at[3], along_y(-2, 1))
        tell(near_sem.at[6], along_y(2, 1))

    @pl.when(jnp.logical_not(second))
    def _():
        pl.semaphore_wait(barrier, 5)
        pass_on()


    def advance(c, state):
        for t in range(CHUNK):
            at = c * CHUNK + t
            if t % KEPT == 0:
                kept[c * (CHUNK // KEPT) + t // KEPT] = state
            state = decay_b * state + u_ref[at][None]
        return state

    zero_state = jnp.zeros((modes, SEG, width), F32)
    ends = loop(1, chunks, BY[2], advance, zero_state)

    pl.semaphore_wait(near_sem.at[1], 2)
    pl.semaphore_wait(near_sem.at[2], 2)
    tell(near_sem.at[4], along_z(-2), along_z(2))
    for copy in halos:
        copy.wait()
    has_before = (ctx > 0).astype(F32)
    top = lax.broadcasted_iota(jnp.int32, (rim, SEG, width), 1) == 0

    def entering(i, tail):
        rows_before = halo[i].astype(F32)[HALO - rim :] * has_before
        spread = jnp.broadcast_to(rows_before[:, None, :], (rim, SEG, width))
        return jnp.where(top, spread, pltpu.roll(tail, 1, 1))

    make_u(0, entering(1, tail_k), entering(2, tail_v))
    first = advance(0, zero_state)
    total = ends + scan_w[3] * first
    for i in range(3):
        total = total + scan_w[i] * pltpu.roll(total, 2**i, 1)
    start = jnp.where(segment >= 1, pltpu.roll(total, 1, 1), 0.0)
    end = total[:, SEG - 1, :]
    device_decay = jnp.exp(lam * (-1.0 * rows))

    inward = pltpu.make_async_remote_copy(
        src_ref=send_state,
        dst_ref=got_state.at[0],
        send_sem=st_s.at[0],
        recv_sem=st_r.at[0],
        device_id=along_ctx(1),
        device_id_type=MESH,
    )
    outward = {
        (k, core): pltpu.make_async_remote_copy(
            src_ref=send_state,
            dst_ref=got_state.at[k],
            send_sem=st_s.at[2 * k + core],
            recv_sem=st_r.at[k],
            device_id=along_y(k, core),
            device_id_type=MESH,
        )
        for k in range(1, y_chips)
        for core in range(2)
    }
    sends = {key: jnp.logical_and(second, my_y < y_chips - key[0]) for key in outward}

    @pl.when(jnp.logical_not(second))
    def _():
        send_state[...] = end.astype(BF16)
        inward.start()

    @pl.when(second)
    def _():
        inward.wait_recv()
        send_state[...] = (device_decay * got_state[0].astype(F32) + end).astype(BF16)

    reaches_on = my_y < y_chips - 3
    pl.when(jnp.logical_and(second, reaches_on))(
        lambda: pl.semaphore_wait(near_sem.at[3], 1)
    )
    by_distance = sorted(outward, key=lambda key: -key[0])
    for key in by_distance:
        if key[0] <= y_chips // 2:
            pl.when(sends[key])(outward[key].start)

    for copy in loads[0]:
        copy.wait()
    w_q = taps_of(0)

    def q_chunk(c, before_q):
        window = jnp.concatenate([before_q, by_step(0, c)], axis=0)
        at = pl.ds(pl.multiple_of(c * CHUNK, CHUNK), CHUNK)
        qs_ref[at] = filtered(w_q, window)
        return window[CHUNK:]

    tail_q = by_step(0, chunks - 1)[CHUNK - rim :]
    loop(0, chunks, BY[3], q_chunk, entering(0, tail_q))

    pl.semaphore_wait(near_sem.at[4], 2)
    tell(near_sem.at[5], along_z(-4), along_z(4))

    response = []
    power_of = coef
    for i in range(CHUNK):
        if i < KEPT:
            response.append(in_all(jnp.sum(power_of, axis=0, keepdims=True)))
        power_of = power_of * decay
        out_pow[i] = per_mode(power_of)
    response[0] = response[0] + in_all(skip_ref[...])

    def y_chunk(c, carry):
        for b in range(CHUNK // KEPT):
            state = kept[c * (CHUNK // KEPT) + b]
            for i in range(KEPT):
                at = c * CHUNK + b * KEPT + i
                y = over_modes(out_pow[i] * state)
                for j in range(i + 1):
                    y = y + response[j] * u_ref[at - j]
                y_ref[at] = y
        return carry

    loop(0, chunks, BY[4], y_chunk, 0)

    lead = jnp.exp(per_mode(lam) * (-1.0 * steps * segment.astype(F32)))
    decay_chunk = per_mode(jnp.exp(lam * (-1.0 * CHUNK)))
    reach = [
        jnp.where(my_y >= k, jnp.exp(lam * (-2.0 * rows * (k - 1))), 0.0)
        for k in range(1, y_chips)
    ]
    pl.when(jnp.logical_and(second, jnp.logical_not(reaches_on)))(
        lambda: pl.semaphore_wait(near_sem.at[3], 1)
    )
    pl.when(second)(lambda: pl.semaphore_wait(near_sem.at[6], 1))
    for key in by_distance[::-1]:
        if key[0] > y_chips // 2:
            pl.when(sends[key])(outward[key].start)
    for k in range(1, y_chips):
        pl.when(my_y >= k)(outward[k, 0].wait_recv)
    terms = [
        jnp.where(my_y >= k, got_state[k].astype(F32), 0.0) * reach[k - 1]
        for k in range(1, y_chips)
    ]
    while len(terms) > 1:
        terms = [sum(terms[i : i + 2]) for i in range(0, len(terms), 2)]
    of_core_0 = jnp.where(second, got_state[0].astype(F32), 0.0)
    incoming = jnp.where(second, device_decay, 1.0) * terms[0] + of_core_0

    lane = lax.broadcasted_iota(jnp.int32, (SEG, LANES), 1)
    gain = in_all(gain_ref[...])

    half = chunks // 2

    def with_power_of(c, power, base):
        place = lane - (c - base) * CHUNK
        for t in range(CHUNK):
            mixed = mix_s[(c + 1) * CHUNK + t]
            power = jnp.where(
                place == t, jnp.sum(mixed * mixed, axis=1, keepdims=True), power
            )
        return power

    def mix_chunk(c, far):
        for t in range(CHUNK):
            at = c * CHUNK + t
            y = y_ref[at] + over_modes(out_pow[t] * far)
            mix_s[at + CHUNK] = qs_ref[at] * y
        return decay_chunk * far

    def mix_group(p, carry, base):
        far, power = carry
        for j in range(GROUP):
            power = with_power_of(GROUP * p + j - 1, power, base)
            far = mix_chunk(GROUP * p + j, far)
            if j == 0:
                far = far + first * (p == 0).astype(F32)
        return far, power

    no_power = jnp.zeros((SEG, LANES), F32)
    mix_s[0:CHUNK] = jnp.zeros((CHUNK, SEG, width), F32)
    far = start + lead * per_mode(incoming)
    far, power_0 = lax.fori_loop(
        0, half // GROUP, functools.partial(mix_group, base=0), (far, no_power)
    )
    power_0 = with_power_of(half - 1, power_0, 0)
    _, power_1 = lax.fori_loop(
        half // GROUP, chunks // GROUP, functools.partial(mix_group, base=half), (far, no_power)
    )
    power_1 = with_power_of(chunks - 1, power_1, half)

    own = jnp.concatenate([power_0, power_1], axis=0)
    send_x[...] = own.astype(BF16)
    over_x = [
        pltpu.make_async_remote_copy(
            src_ref=send_x,
            dst_ref=got_x.at[k],
            send_sem=x_s,
            recv_sem=x_r,
            device_id=along_x(k),
            device_id_type=MESH,
        )
        for k in range(1, X_CHIPS)
    ]
    for copy in over_x:
        copy.start()

    def relayout(c, carry):
        at = pl.ds(pl.multiple_of((c + 1) * CHUNK, CHUNK), CHUNK)
        by_segment = jnp.swapaxes(mix_s[at] * gain, 0, 1)
        for s in range(SEG):
            to = pl.multiple_of(s * steps + c * CHUNK, CHUNK)
            mix_ref[pl.ds(to, CHUNK), :] = by_segment[s]
        return carry

    loop(0, chunks, BY[5], relayout, 0)
    pl.when(jnp.logical_not(second))(inward.wait_send)
    for key in outward:
        pl.when(sends[key])(outward[key].wait_send)
    all_of(got_x, x_r)
    own = own + sum(got_x[k].astype(F32) for k in range(1, X_CHIPS))
    send_z[...] = own.astype(BF16)
    over_z = [
        pltpu.make_async_remote_copy(
            src_ref=send_z,
            dst_ref=got_z.at[k],
            send_sem=z_s,
            recv_sem=z_r,
            device_id=along_z(k),
            device_id_type=MESH,
        )
        for k in range(1, z_chips)
    ]
    pl.semaphore_wait(near_sem.at[5], 2)
    for copy in over_z:
        copy.start()
    all_of(got_x, x_s)
    all_of(got_z, z_s)
    all_of(got_z, z_r)
    terms = [own] + [got_z[k].astype(F32) for k in range(1, z_chips)]
    while len(terms) > 1:
        terms = [sum(terms[i : i + 2]) for i in range(0, len(terms), 2)]
    sum_ref[...] = terms[0]


def finish(channels, mix_ref, sum_ref, out_hbm, out_v, out_sem):
    groups = sum_ref.shape[0]
    scale = lax.rsqrt(sum_ref[...] * (1.0 / channels) + 1e-05)
    halves = groups // SEG
    outs = []
    for g in range(groups):
        row = (g % halves) * SEG + g // halves
        spread = jnp.broadcast_to(scale[row : row + 1], (LANES, LANES)).T
        at = pl.ds(g * LANES, LANES)
        out_v[at, :] = (mix_ref[at, :] * spread).astype(BF16)
        if g % 4 == 3:
            span = pl.ds((g - 3) * LANES, 4 * LANES)
            copy = pltpu.make_async_copy(out_v.at[span], out_hbm.at[span], out_sem.at[g // 4])
            copy.start()
            outs.append(copy)
    for copy in outs:
        copy.wait()


def shards(n_ctx, n_chan, queries, keys_in, values_in, short_weights, decay_rates, residues, skip_term, out_gain):
    rows, width = queries.shape[1:]
    taps, modes = short_weights.shape[1], decay_rates.shape[0]
    steps, groups = rows // SEG, rows // LANES
    z_chips = n_chan // X_CHIPS
    dma = pltpu.SemaphoreType.DMA
    vmem = pl.BlockSpec(memory_space=pltpu.VMEM)
    hbm = pl.BlockSpec(memory_space=pltpu.HBM)
    mixed, sums = pl.pallas_call(
        functools.partial(body, (n_ctx, n_chan, width, taps, modes)),
        out_shape=(
            jax.ShapeDtypeStruct((rows, width), F32),
            jax.ShapeDtypeStruct((groups, LANES), F32),
        ),
        in_specs=[hbm] * 8,
        out_specs=(vmem, vmem),
        scratch_shapes=[
            pltpu.VMEM((3, SEG, steps, width), BF16),
            pltpu.VMEM((3, taps, width), F32),
            pltpu.VMEM((modes, width), F32),
            pltpu.VMEM((modes, width), F32),
            pltpu.VMEM((1, width), F32),
            pltpu.VMEM((1, width), F32),
            pltpu.VMEM((3, HALO, width), BF16),
            pltpu.VMEM((steps, SEG, width), F32),
            pltpu.VMEM((steps, SEG, width), F32),
            pltpu.VMEM((steps, SEG, width), F32),
            pltpu.VMEM((steps + CHUNK, SEG, width), F32),
            pltpu.VMEM((steps // KEPT, modes, SEG, width), F32),
            pltpu.VMEM((CHUNK, modes, SEG, width), F32),
            pltpu.VMEM((4, modes, SEG, width), F32),
            pltpu.VMEM((modes, width), BF16),
            pltpu.VMEM((n_ctx // 2, modes, width), BF16),
            pltpu.VMEM((groups, LANES), BF16),
            pltpu.VMEM((X_CHIPS, groups, LANES), BF16),
            pltpu.VMEM((groups, LANES), BF16),
            pltpu.VMEM((z_chips, groups, LANES), BF16),
            dma((3, 2)),
            dma((5,)),
            dma((3,)),
            dma((3,)),
            dma((n_ctx,)),
            dma((n_ctx // 2,)),
            dma,
            dma,
            dma,
            dma,
            pltpu.SemaphoreType.REGULAR((7,)),
        ],
        compiler_params=pltpu.CompilerParams(
            collective_id=0, has_side_effects=True, vmem_limit_bytes=24 << 20
        ),
        name="hyena",
    )(
        *(
            pltpu.with_memory_space_constraint(x, pltpu.HBM)
            for x in (
                queries.reshape(SEG, steps, width),
                keys_in.reshape(SEG, steps, width),
                values_in.reshape(SEG, steps, width),
                short_weights,
                decay_rates,
                residues,
                skip_term[None],
                out_gain[None],
            )
        )
    )
    out = pl.pallas_call(
        functools.partial(finish, width * n_chan),
        out_shape=jax.ShapeDtypeStruct((rows, width), BF16),
        in_specs=[vmem, vmem],
        out_specs=hbm,
        scratch_shapes=[pltpu.VMEM((rows, width), BF16), dma((groups // 4,))],
        compiler_params=pltpu.CompilerParams(vmem_limit_bytes=8 << 20),
        name="finish",
    )(mixed, sums)
    return out[None]


def solution(mesh):
    placed = (
        P(None, "ctx", "chan"),
        P(None, "ctx", "chan"),
        P(None, "ctx", "chan"),
        P(None, None, "chan"),
        P(None, "chan"),
        P(None, "chan"),
        P("chan"),
        P("chan"),
    )
    return jax.shard_map(
        functools.partial(shards, mesh.shape["ctx"], mesh.shape["chan"]),
        mesh=mesh,
        in_specs=placed,
        out_specs=P(None, "ctx", "chan"),
        check_vma=False,
    )
```

```python
import functools

import jax
import jax.numpy as jnp
from jax import lax
from jax.experimental import pallas as pl
from jax.experimental.pallas import tpu as pltpu
from jax.sharding import PartitionSpec as P

MESH = pl.DeviceIdType.MESH
F32 = jnp.float32
BF16 = jnp.bfloat16
SEG = 8
LANES = 128
CHUNK = 16
KEPT = 4
GROUP = 8
BY = (7, 8, 15, 4, 8, 4)
HALO = 16
X_CHIPS = 4


def expm1_of_minus(x):
    series = jnp.full_like(x, 1.0 / 40320.0)
    for factor in (5040.0, 720.0, 120.0, 24.0, 6.0, 2.0, 1.0):
        series = 1.0 / factor - x * series
    return jnp.where(x < 0.25, x * series, 1.0 - jnp.exp(-x))


def per_mode(rows):
    return jnp.broadcast_to(rows[:, None, :], (rows.shape[0], SEG, rows.shape[1]))


def loop(first, last, by, step, carry):
    def some(g, carry):
        for j in range(by):
            carry = step(first + g * by + j, carry)
        return carry

    return lax.fori_loop(0, (last - first) // by, some, carry)


def over_modes(terms):
    while terms.shape[0] > 1:
        half = terms.shape[0] // 2
        terms = terms[:half] + terms[half:]
    return terms[0]


def in_all(row):
    return jnp.broadcast_to(row, (SEG, row.shape[-1]))


def body(
    sizes,
    q_hbm,
    k_hbm,
    v_hbm,
    w_hbm,
    lam_hbm,
    res_hbm,
    skip_hbm,
    gain_hbm,
    mix_ref,
    sum_ref,
    raw,
    w_ref,
    lam_ref,
    res_ref,
    skip_ref,
    gain_ref,
    halo,
    u_ref,
    qs_ref,
    y_ref,
    mix_s,
    kept,
    out_pow,
    scan_w,
    send_state,
    got_state,
    send_x,
    got_x,
    send_z,
    got_z,
    in_sem,
    par_sem,
    halo_s,
    halo_r,
    st_s,
    st_r,
    x_s,
    x_r,
    z_s,
    z_r,
    near_sem,
):
    n_ctx, n_chan, width, taps, modes = sizes
    steps = q_hbm.shape[1]
    rows = SEG * steps
    chunks = steps // CHUNK
    rim = taps - 1
    z_chips = n_chan // X_CHIPS
    ctx = lax.axis_index("ctx")
    chan = lax.axis_index("chan")
    my_x, my_z = lax.div(chan, z_chips), lax.rem(chan, z_chips)
    y_chips = n_ctx // 2
    my_y, my_core = lax.div(ctx, 2), lax.rem(ctx, 2)

    def along_ctx(k):
        return (lax.rem(ctx + k, n_ctx), chan)

    def along_y(k, core):
        return (2 * lax.rem(my_y + (k + y_chips), y_chips) + core, chan)

    def along_x(k):
        return (ctx, lax.rem(my_x + (k + X_CHIPS), X_CHIPS) * z_chips + my_z)

    def along_z(k):
        return (ctx, my_x * z_chips + lax.rem(my_z + (k + z_chips), z_chips))

    def all_of(got, *sems):
        part = got.at[pl.ds(1, got.shape[0] - 1)]
        for sem in sems:
            pltpu.make_async_copy(part, part, sem).wait()

    def tell(sem, *others):
        for other in others:
            pl.semaphore_signal(sem, inc=1, device_id=other, device_id_type=MESH)

    streams = (q_hbm, k_hbm, v_hbm)
    params = [
        pltpu.make_async_copy(src, dst, par_sem.at[i])
        for i, (src, dst) in enumerate(
            (
                (w_hbm, w_ref),
                (lam_hbm, lam_ref),
                (res_hbm, res_ref),
                (skip_hbm, skip_ref),
                (gain_hbm, gain_ref),
            )
        )
    ]
    loads = [
        [
            pltpu.make_async_copy(
                streams[i].at[:, pl.ds(h * (steps // 2), steps // 2)],
                raw.at[i, :, pl.ds(h * (steps // 2), steps // 2)],
                in_sem.at[i, h],
            )
            for h in range(2)
        ]
        for i in range(3)
    ]
    for copy in params:
        copy.start()
    for h in range(2):
        loads[1][h].start()
        loads[2][h].start()
    for h in range(2):
        loads[0][h].start()

    barrier = pltpu.get_barrier_semaphore()
    second = my_core == 1
    pl.when(second)(lambda: tell(barrier, along_y(1, 1)))
    tell(
        barrier,
        along_y(0, 1 - my_core),
        along_y(-1, 1),
        along_x(-1),
        along_x(1),
        along_z(-1),
        along_z(1),
    )
    for copy in params:
        copy.wait()

    lam = lam_ref[...]
    coef = res_ref[...] * jnp.sqrt(expm1_of_minus(2.0 * lam))
    decay = 1.0 - expm1_of_minus(lam)
    decay_b = per_mode(decay)

    segment = lax.broadcasted_iota(jnp.int32, (modes, SEG, width), 1)
    for i in range(3):
        weight = per_mode(jnp.exp(lam * (-1.0 * steps * 2**i)))
        scan_w[i] = jnp.where(segment >= 2**i, weight, 0.0)
    scan_w[3] = per_mode(jnp.exp(lam * (-1.0 * (steps - CHUNK))))

    def by_step(i, c):
        part = raw[i, :, pl.ds(pl.multiple_of(c * CHUNK, CHUNK), CHUNK), :]
        return jnp.swapaxes(part.astype(F32), 0, 1)

    def taps_of(i):
        return [in_all(w_ref[i, j : j + 1, :]) for j in range(taps)]

    def filtered(weights, window):
        total = weights[0][None] * window[rim:]
        for j in range(1, taps):
            total = total + weights[j][None] * window[rim - j : rim - j + CHUNK]
        return total

    def make_u(c, before_k, before_v):
        window_k = jnp.concatenate([before_k, by_step(1, c)], axis=0)
        window_v = jnp.concatenate([before_v, by_step(2, c)], axis=0)
        at = pl.ds(pl.multiple_of(c * CHUNK, CHUNK), CHUNK)
        u_ref[at] = filtered(w_k, window_k) * filtered(w_v, window_v)
        return window_k[CHUNK:], window_v[CHUNK:]

    def u_chunk(c, before):
        return make_u(c, *before)

    for i in (1, 2):
        loads[i][0].wait()
    w_k, w_v = taps_of(1), taps_of(2)
    first_k, first_v = by_step(1, 0)[CHUNK - rim :], by_step(2, 0)[CHUNK - rim :]

    halos = [
        pltpu.make_async_remote_copy(
            src_ref=streams[i].at[SEG - 1, pl.ds(steps - HALO, HALO)],
            dst_ref=halo.at[i],
            send_sem=halo_s.at[i],
            recv_sem=halo_r.at[i],
            device_id=along_ctx(1),
            device_id_type=MESH,
        )
        for i in range(3)
    ]

    def pass_on():
        for copy in halos:
            copy.start()
        tell(near_sem.at[1], along_x(-1), along_x(1))
        tell(near_sem.at[2], along_z(-1), along_z(1))

    @pl.when(second)
    def _():
        pl.semaphore_wait(barrier, 8)
        tell(near_sem.at[0], along_y(-1, 1), along_y(1, 1))
        pass_on()

    before = loop(1, chunks // 2, BY[0], u_chunk, (first_k, first_v))

    for i in (1, 2):
        loads[i][1].wait()
    tail_k, tail_v = loop(chunks // 2, chunks, BY[1], u_chunk, before)

    @pl.when(second)
    def _():
        pl.semaphore_wait(near_sem.at[0], 2)
        tell(near_sem.at[3], along_y(-2, 1), along_y(2, 1))

    @pl.when(jnp.logical_not(second))
    def _():
        pl.semaphore_wait(barrier, 5)
        pass_on()


    def advance(c, state):
        for t in range(CHUNK):
            at = c * CHUNK + t
            if t % KEPT == 0:
                kept[c * (CHUNK // KEPT) + t // KEPT] = state
            state = decay_b * state + u_ref[at][None]
        return state

    zero_state = jnp.zeros((modes, SEG, width), F32)
    ends = loop(1, chunks, BY[2], advance, zero_state)

    pl.semaphore_wait(near_sem.at[1], 2)
    pl.semaphore_wait(near_sem.at[2], 2)
    tell(near_sem.at[4], along_z(-2), along_z(2))
    for copy in halos:
        copy.wait()
    has_before = (ctx > 0).astype(F32)
    top = lax.broadcasted_iota(jnp.int32, (rim, SEG, width), 1) == 0

    def entering(i, tail):
        rows_before = halo[i].astype(F32)[HALO - rim :] * has_before
        spread = jnp.broadcast_to(rows_before[:, None, :], (rim, SEG, width))
        return jnp.where(top, spread, pltpu.roll(tail, 1, 1))

    make_u(0, entering(1, tail_k), entering(2, tail_v))
    first = advance(0, zero_state)
    total = ends + scan_w[3] * first
    for i in range(3):
        total = total + scan_w[i] * pltpu.roll(total, 2**i, 1)
    start = jnp.where(segment >= 1, pltpu.roll(total, 1, 1), 0.0)
    end = total[:, SEG - 1, :]
    device_decay = jnp.exp(lam * (-1.0 * rows))

    inward = pltpu.make_async_remote_copy(
        src_ref=send_state,
        dst_ref=got_state.at[0],
        send_sem=st_s.at[0],
        recv_sem=st_r.at[0],
        device_id=along_ctx(1),
        device_id_type=MESH,
    )
    outward = {
        (k, core): pltpu.make_async_remote_copy(
            src_ref=send_state,
            dst_ref=got_state.at[k],
            send_sem=st_s.at[2 * k + core],
            recv_sem=st_r.at[k],
            device_id=along_y(k, core),
            device_id_type=MESH,
        )
        for k in range(1, y_chips)
        for core in range(2)
    }
    sends = {key: jnp.logical_and(second, my_y < y_chips - key[0]) for key in outward}

    @pl.when(jnp.logical_not(second))
    def _():
        send_state[...] = end.astype(BF16)
        inward.start()

    @pl.when(second)
    def _():
        inward.wait_recv()
        send_state[...] = (device_decay * got_state[0].astype(F32) + end).astype(BF16)

    reaches_on = my_y < y_chips - 3
    pl.when(jnp.logical_and(second, reaches_on))(
        lambda: pl.semaphore_wait(near_sem.at[3], 2)
    )
    for key in sorted(outward, key=lambda key: abs(key[0] - y_chips // 2)):
        pl.when(sends[key])(outward[key].start)

    for copy in loads[0]:
        copy.wait()
    w_q = taps_of(0)

    def q_chunk(c, before_q):
        window = jnp.concatenate([before_q, by_step(0, c)], axis=0)
        at = pl.ds(pl.multiple_of(c * CHUNK, CHUNK), CHUNK)
        qs_ref[at] = filtered(w_q, window)
        return window[CHUNK:]

    tail_q = by_step(0, chunks - 1)[CHUNK - rim :]
    loop(0, chunks, BY[3], q_chunk, entering(0, tail_q))

    pl.semaphore_wait(near_sem.at[4], 2)
    tell(near_sem.at[5], along_z(-4), along_z(4))

    response = []
    power_of = coef
    for i in range(CHUNK):
        if i < KEPT:
            response.append(in_all(jnp.sum(power_of, axis=0, keepdims=True)))
        power_of = power_of * decay
        out_pow[i] = per_mode(power_of)
    response[0] = response[0] + in_all(skip_ref[...])

    def y_chunk(c, carry):
        for b in range(CHUNK // KEPT):
            state = kept[c * (CHUNK // KEPT) + b]
            for i in range(KEPT):
                at = c * CHUNK + b * KEPT + i
                y = over_modes(out_pow[i] * state)
                for j in range(i + 1):
                    y = y + response[j] * u_ref[at - j]
                y_ref[at] = y
        return carry

    loop(0, chunks, BY[4], y_chunk, 0)

    lead = jnp.exp(per_mode(lam) * (-1.0 * steps * segment.astype(F32)))
    decay_chunk = per_mode(jnp.exp(lam * (-1.0 * CHUNK)))
    reach = [
        jnp.where(my_y >= k, jnp.exp(lam * (-2.0 * rows * (k - 1))), 0.0)
        for k in range(1, y_chips)
    ]
    pl.when(jnp.logical_and(second, jnp.logical_not(reaches_on)))(
        lambda: pl.semaphore_wait(near_sem.at[3], 2)
    )
    for k in range(1, y_chips):
        pl.when(my_y >= k)(outward[k, 0].wait_recv)
    terms = [
        jnp.where(my_y >= k, got_state[k].astype(F32), 0.0) * reach[k - 1]
        for k in range(1, y_chips)
    ]
    while len(terms) > 1:
        terms = [sum(terms[i : i + 2]) for i in range(0, len(terms), 2)]
    of_core_0 = jnp.where(second, got_state[0].astype(F32), 0.0)
    incoming = jnp.where(second, device_decay, 1.0) * terms[0] + of_core_0

    lane = lax.broadcasted_iota(jnp.int32, (SEG, LANES), 1)
    gain = in_all(gain_ref[...])

    half = chunks // 2

    def with_power_of(c, power, base):
        place = lane - (c - base) * CHUNK
        for t in range(CHUNK):
            mixed = mix_s[(c + 1) * CHUNK + t]
            power = jnp.where(
                place == t, jnp.sum(mixed * mixed, axis=1, keepdims=True), power
            )
        return power

    def mix_chunk(c, far):
        for t in range(CHUNK):
            at = c * CHUNK + t
            y = y_ref[at] + over_modes(out_pow[t] * far)
            mix_s[at + CHUNK] = qs_ref[at] * y
        return decay_chunk * far

    def mix_group(p, carry, base):
        far, power = carry
        for j in range(GROUP):
            power = with_power_of(GROUP * p + j - 1, power, base)
            far = mix_chunk(GROUP * p + j, far)
            if j == 0:
                far = far + first * (p == 0).astype(F32)
        return far, power

    no_power = jnp.zeros((SEG, LANES), F32)
    mix_s[0:CHUNK] = jnp.zeros((CHUNK, SEG, width), F32)
    far = start + lead * per_mode(incoming)
    far, power_0 = lax.fori_loop(
        0, half // GROUP, functools.partial(mix_group, base=0), (far, no_power)
    )
    power_0 = with_power_of(half - 1, power_0, 0)
    _, power_1 = lax.fori_loop(
        half // GROUP, chunks // GROUP, functools.partial(mix_group, base=half), (far, no_power)
    )
    power_1 = with_power_of(chunks - 1, power_1, half)

    own = jnp.concatenate([power_0, power_1], axis=0)
    send_x[...] = own.astype(BF16)
    over_x = [
        pltpu.make_async_remote_copy(
            src_ref=send_x,
            dst_ref=got_x.at[k],
            send_sem=x_s,
            recv_sem=x_r,
            device_id=along_x(k),
            device_id_type=MESH,
        )
        for k in range(1, X_CHIPS)
    ]
    for copy in over_x:
        copy.start()

    def relayout(c, carry):
        at = pl.ds(pl.multiple_of((c + 1) * CHUNK, CHUNK), CHUNK)
        by_segment = jnp.swapaxes(mix_s[at] * gain, 0, 1)
        for s in range(SEG):
            to = pl.multiple_of(s * steps + c * CHUNK, CHUNK)
            mix_ref[pl.ds(to, CHUNK), :] = by_segment[s]
        return carry

    loop(0, chunks, BY[5], relayout, 0)
    pl.when(jnp.logical_not(second))(inward.wait_send)
    for key in outward:
        pl.when(sends[key])(outward[key].wait_send)
    all_of(got_x, x_r)
    own = own + sum(got_x[k].astype(F32) for k in range(1, X_CHIPS))
    send_z[...] = own.astype(BF16)
    over_z = [
        pltpu.make_async_remote_copy(
            src_ref=send_z,
            dst_ref=got_z.at[k],
            send_sem=z_s,
            recv_sem=z_r,
            device_id=along_z(k),
            device_id_type=MESH,
        )
        for k in range(1, z_chips)
    ]
    pl.semaphore_wait(near_sem.at[5], 2)
    for copy in over_z:
        copy.start()
    all_of(got_x, x_s)
    all_of(got_z, z_s)
    all_of(got_z, z_r)
    terms = [own] + [got_z[k].astype(F32) for k in range(1, z_chips)]
    while len(terms) > 1:
        terms = [sum(terms[i : i + 2]) for i in range(0, len(terms), 2)]
    sum_ref[...] = terms[0]


def finish(channels, mix_ref, sum_ref, out_hbm, out_v, out_sem):
    groups = sum_ref.shape[0]
    scale = lax.rsqrt(sum_ref[...] * (1.0 / channels) + 1e-05)
    halves = groups // SEG
    outs = []
    for g in range(groups):
        row = (g % halves) * SEG + g // halves
        spread = jnp.broadcast_to(scale[row : row + 1], (LANES, LANES)).T
        at = pl.ds(g * LANES, LANES)
        out_v[at, :] = (mix_ref[at, :] * spread).astype(BF16)
        if g % 4 == 3:
            span = pl.ds((g - 3) * LANES, 4 * LANES)
            copy = pltpu.make_async_copy(out_v.at[span], out_hbm.at[span], out_sem.at[g // 4])
            copy.start()
            outs.append(copy)
    for copy in outs:
        copy.wait()


def shards(n_ctx, n_chan, queries, keys_in, values_in, short_weights, decay_rates, residues, skip_term, out_gain):
    rows, width = queries.shape[1:]
    taps, modes = short_weights.shape[1], decay_rates.shape[0]
    steps, groups = rows // SEG, rows // LANES
    z_chips = n_chan // X_CHIPS
    dma = pltpu.SemaphoreType.DMA
    vmem = pl.BlockSpec(memory_space=pltpu.VMEM)
    hbm = pl.BlockSpec(memory_space=pltpu.HBM)
    mixed, sums = pl.pallas_call(
        functools.partial(body, (n_ctx, n_chan, width, taps, modes)),
        out_shape=(
            jax.ShapeDtypeStruct((rows, width), F32),
            jax.ShapeDtypeStruct((groups, LANES), F32),
        ),
        in_specs=[hbm] * 8,
        out_specs=(vmem, vmem),
        scratch_shapes=[
            pltpu.VMEM((3, SEG, steps, width), BF16),
            pltpu.VMEM((3, taps, width), F32),
            pltpu.VMEM((modes, width), F32),
            pltpu.VMEM((modes, width), F32),
            pltpu.VMEM((1, width), F32),
            pltpu.VMEM((1, width), F32),
            pltpu.VMEM((3, HALO, width), BF16),
            pltpu.VMEM((steps, SEG, width), F32),
            pltpu.VMEM((steps, SEG, width), F32),
            pltpu.VMEM((steps, SEG, width), F32),
            pltpu.VMEM((steps + CHUNK, SEG, width), F32),
            pltpu.VMEM((steps // KEPT, modes, SEG, width), F32),
            pltpu.VMEM((CHUNK, modes, SEG, width), F32),
            pltpu.VMEM((4, modes, SEG, width), F32),
            pltpu.VMEM((modes, width), BF16),
            pltpu.VMEM((n_ctx // 2, modes, width), BF16),
            pltpu.VMEM((groups, LANES), BF16),
            pltpu.VMEM((X_CHIPS, groups, LANES), BF16),
            pltpu.VMEM((groups, LANES), BF16),
            pltpu.VMEM((z_chips, groups, LANES), BF16),
            dma((3, 2)),
            dma((5,)),
            dma((3,)),
            dma((3,)),
            dma((n_ctx,)),
            dma((n_ctx // 2,)),
            dma,
            dma,
            dma,
            dma,
            pltpu.SemaphoreType.REGULAR((6,)),
        ],
        compiler_params=pltpu.CompilerParams(
            collective_id=0, has_side_effects=True, vmem_limit_bytes=24 << 20
        ),
        name="hyena",
    )(
        *(
            pltpu.with_memory_space_constraint(x, pltpu.HBM)
            for x in (
                queries.reshape(SEG, steps, width),
                keys_in.reshape(SEG, steps, width),
                values_in.reshape(SEG, steps, width),
                short_weights,
                decay_rates,
                residues,
                skip_term[None],
                out_gain[None],
            )
        )
    )
    out = pl.pallas_call(
        functools.partial(finish, width * n_chan),
        out_shape=jax.ShapeDtypeStruct((rows, width), BF16),
        in_specs=[vmem, vmem],
        out_specs=hbm,
        scratch_shapes=[pltpu.VMEM((rows, width), BF16), dma((groups // 4,))],
        compiler_params=pltpu.CompilerParams(vmem_limit_bytes=8 << 20),
        name="finish",
    )(mixed, sums)
    return out[None]


def solution(mesh):
    placed = (
        P(None, "ctx", "chan"),
        P(None, "ctx", "chan"),
        P(None, "ctx", "chan"),
        P(None, None, "chan"),
        P(None, "chan"),
        P(None, "chan"),
        P("chan"),
        P("chan"),
    )
    return jax.shard_map(
        functools.partial(shards, mesh.shape["ctx"], mesh.shape["chan"]),
        mesh=mesh,
        in_specs=placed,
        out_specs=P(None, "ctx", "chan"),
        check_vma=False,
    )
```
